32 devices in a mesh: ctx: 8 (over z, y), hd: 4 (over x, core).
Axes of the slice: x: 2, y: 2, z: 4, core: 2. Of those that a mesh axis runs over, the one named last changes fastest.
Arguments:
- hidden_in: bfloat16 [2048, 2048], P('ctx'), may hold values from -6 to 6
- q_latent: bfloat16 [2048, 4096], P('ctx', 'hd'), may hold values from -18 to 18
- q_rotary: bfloat16 [2048, 512], P('ctx', 'hd'), may hold values from -6 to 6
- latent: bfloat16 [512, 2048], P(None, 'ctx'), may hold values from -6 to 6
- k_rotary: bfloat16 [64, 2048], P(None, 'ctx'), may hold values from -6 to 6
- w_value: bfloat16 [8, 512, 128], P('hd'), may hold values from -0.25 to 0.25
- w_output: bfloat16 [1024, 2048], P('hd'), may hold values from -0.1875 to 0.1875
- ffn_gain: float32 [2048], replicated, may hold values from 0.5 to 2
- w_gate: bfloat16 [8, 2048, 1408], P('ctx', None, 'hd'), may hold values from -0.125 to 0.125
- w_up: bfloat16 [8, 2048, 1408], P('ctx', None, 'hd'), may hold values from -0.125 to 0.125
- w_down: bfloat16 [8, 1408, 2048], P('ctx', 'hd'), may hold values from -0.15625 to 0.15625
- expert_ids: int32 [2048, 2], P('ctx'), may hold values from 0 to 7, all different within a row; in each aligned block of 256 rows (0 to 255, 256 to 511, ...) at most 96 rows name the same one
- gate_index: int32 [2048, 2], P('ctx'), may hold values from 0 to 63
- gate_table: float32 [64], replicated, may hold values from 0.1 to 1
Outputs:
- mixed: bfloat16 [2048, 2048], P('ctx', 'hd')
The draws below stay inside these ranges and needn't reach their ends.
Inputs may be any that keep to these rules, and one draw needn't show every extreme that they name: `expert_ids`: each row names 2 different experts; in the rows of one device (aligned blocks of 256 rows) no expert is named by more than 96 entries.
All inputs are finite; a program needn't handle non-finite values.
Results may differ from the reference program's by a relative error of at most 0.013.
Values may be sent and summed in bfloat16 or wider, within the bound.
A program may use at most 192 MiB of HBM per device.

```python
import math
import jax
import jax.numpy as jnp
import numpy as np
from jax import lax

D = 2048
KVR = 512
ROPE = 64
NOPE = 128
VD = 128
FF = 1408
HEADS = 8
TOPK = 2
GATES = 64
TOK_DEV = 256
EXPERTS = 8
SEQ = 2048
CAP = 96
N_CTX = 8


def draw_latent(key, part):
    inner = jax.random.fold_in(key, 11)
    values = jnp.clip(jax.random.normal(inner, (SEQ, KVR), jnp.float32), -6.0, 6.0)
    return values.T.astype(jnp.bfloat16)


def draw_q_latent(key, part):
    inner = jax.random.fold_in(key, 13)
    values = jnp.clip(2.0 * jax.random.normal(inner, (SEQ, HEADS * KVR), jnp.float32), -12.0, 12.0)
    return values.astype(jnp.bfloat16)


def draw_q_rotary(key, part):
    inner = jax.random.fold_in(key, 17)
    values = jnp.clip(jax.random.normal(inner, (SEQ, HEADS * ROPE), jnp.float32), -6.0, 6.0)
    return values.astype(jnp.bfloat16)


def with_ends(values, key, least, top_value):
    shape = values.shape
    place = [jax.random.randint(jax.random.fold_in(key, axis), (), 0, shape[axis]) for axis in range(len(shape))]
    values = values.at[tuple(place)].set(least)
    longest = shape.index(max(shape))
    place[longest] = (place[longest] + 1) % shape[longest]
    return values.at[tuple(place)].set(top_value)


def steps_of(key, extent, shards, low, top_value):
    def one(dim, blocks):
        heights = jax.random.uniform(jax.random.fold_in(jax.random.fold_in(key, 6), dim), (blocks,), jnp.float32, low / len(shards), top_value / len(shards))
        return jnp.repeat(jnp.exp(heights), extent[dim] // blocks).reshape((-1,) + (1,) * (len(extent) - dim - 1))

    level = one(*shards[0])
    for cut in shards[1:]:
        level = level * one(*cut)
    return level


def shared_out(rng, own, number, rows, count, top, bound, lean):
    sequence = jax.random.permutation(rng, count)
    packed, common = portions_of(count, rows * top, bound, lean, True), portions_of(count, rows * top, bound, lean, False)
    places = jnp.arange(count)

    def named(sizes, rotation):
        used = int((sizes > 0).sum())
        fixed = max(1, used // 4)
        passed = fixed + (places - fixed + rotation * (used - fixed)) % max(1, count - fixed)
        return jnp.zeros((count,), jnp.int32).at[sequence[jnp.where(places < fixed, places, passed)]].set(jnp.asarray(sizes, jnp.int32))

    sizes = jnp.where(number % 4 == 0, named(packed, number // 4), named(common, number - number // 4 - 1))
    mixed = jax.random.permutation(jax.random.fold_in(own, 3), count)
    donor, taker = mixed[0:count // 2 * 2:2], mixed[1:count // 2 * 2:2]
    room = jnp.minimum(sizes[donor] - 1, bound - sizes[taker]) // 2
    room = jnp.where((donor == sequence[0]) | (taker == sequence[0]) | (sizes[taker] == 0), 0, jnp.maximum(room, 0))
    passed = jax.random.randint(jax.random.fold_in(own, 4), (count // 2,), 0, 1 << 20) % (room + 1)
    sizes = sizes.at[donor].add(-passed).at[taker].add(passed)
    members = jnp.searchsorted(jnp.cumsum(sizes), jnp.arange(rows * top), side="right").astype(jnp.int32)
    table = members.reshape(top, rows).T
    table = table[jax.random.permutation(jax.random.fold_in(own, 1), rows)]
    rotation = jax.random.randint(jax.random.fold_in(own, 2), (rows, 1), 0, top)
    return jnp.take_along_axis(table, (jnp.arange(top)[None, :] + rotation) % top, axis=1)


def portions_of(amount, total, most, lean, full):
    portions = [(1 << 20) // math.isqrt(rank ** lean) + 1 for rank in range(1, amount + 1)]
    largest = most if full else min(most, max(-(-total // amount), total * portions[0] // sum(portions)))
    least = 1 if total - largest >= amount - 1 else 0
    given, surplus = [largest] + [least] * (amount - 1), total - largest - least * (amount - 1)
    while surplus > 0:
        free = [i for i in range(1, amount) if given[i] < largest] or [i for i in range(1, amount) if given[i] < most]
        whole, budget = sum([portions[i] for i in free]), surplus
        for i in free:
            more = min(most - given[i], max(1, budget * portions[i] // whole), surplus)
            given[i] = given[i] + more
            surplus = surplus - more
    return np.array(given)


def noise(rng, dims, deviation, most, shards=(), kind=jnp.bfloat16):
    factor_of = steps_of(rng, dims, shards, -0.22, 0.18) if shards else 1.0
    drawn = jax.random.normal(rng, dims, jnp.float32) * deviation * factor_of
    return jnp.minimum(jnp.maximum(drawn, -most), most).astype(kind)


def setup_inputs(seed: int = 0) -> dict:
    key_of = jax.random.split(jax.random.key(seed), 15)
    hidden_in = noise(key_of[0], (SEQ, D), 1.0, 6.0, ((0, 8),))
    q_latent = draw_q_latent(jax.random.fold_in(key_of[14], 71), 0)
    q_rotary = draw_q_rotary(jax.random.fold_in(key_of[14], 71), 0)
    latent = draw_latent(jax.random.fold_in(key_of[14], 71), 0)
    k_rotary = noise(key_of[4], (ROPE, SEQ), 1.0, 6.0, ((1, 8),))
    w_value = noise(key_of[5], (HEADS, KVR, VD), KVR ** -0.5, 0.25, ((0, 4),))
    w_output = noise(key_of[6], (HEADS * VD, D), (HEADS * VD) ** -0.5, 0.1875, ((0, 4),))
    ffn_gain = jnp.clip(jnp.exp(jax.random.uniform(key_of[7], (D,), jnp.float32, math.log(0.5), math.log(2.0))), 0.5, 2.0)
    w_gate = noise(key_of[8], (EXPERTS, D, FF), D ** -0.5, 0.125, ((0, 8), (2, 4)))
    w_up = noise(key_of[9], (EXPERTS, D, FF), D ** -0.5, 0.125, ((0, 8), (2, 4)))
    w_down = noise(key_of[10], (EXPERTS, FF, D), FF ** -0.5, 0.15625, ((0, 8), (1, 4)))
    expert_ids_keys = jax.random.split(jax.random.fold_in(key_of[11], 1), SEQ // TOK_DEV)
    expert_ids_turns = jax.random.permutation(jax.random.fold_in(key_of[11], 3), SEQ // TOK_DEV)
    expert_ids = jax.vmap(lambda own, number: shared_out(jax.random.fold_in(key_of[11], 2), own, number, TOK_DEV, EXPERTS, TOPK, CAP, 2))(expert_ids_keys, expert_ids_turns).reshape((SEQ, TOPK))
    gate_index = with_ends(jax.random.randint(key_of[12], (SEQ, TOPK), 0, GATES), jax.random.fold_in(key_of[12], 1), 0, GATES - 1).astype(jnp.int32)
    gate_table = jnp.clip(jnp.exp(jax.random.uniform(key_of[13], (GATES,), jnp.float32, math.log(0.1), math.log(1.0))), 0.1, 1.0)
    return {"hidden_in": hidden_in, "q_latent": q_latent, "q_rotary": q_rotary, "latent": latent, "k_rotary": k_rotary, "w_value": w_value, "w_output": w_output, "ffn_gain": ffn_gain, "w_gate": w_gate, "w_up": w_up, "w_down": w_down, "expert_ids": expert_ids, "gate_index": gate_index, "gate_table": gate_table}


def attention_rows(q_latent, q_rotary, latent, k_rotary):
    block = math.gcd(SEQ, 512)
    blocks = SEQ // block
    score_scale = 1.0 / math.sqrt(NOPE + ROPE)
    queries = q_latent.reshape(SEQ, HEADS, KVR).astype(jnp.float32)
    rotary = q_rotary.reshape(SEQ, HEADS, ROPE).astype(jnp.float32)
    latent_wide = latent.astype(jnp.float32)
    rope_wide = k_rotary.astype(jnp.float32)

    def one_block(index_block):
        row_start = (index_block * block).astype(jnp.int32)
        query_block = lax.dynamic_slice_in_dim(queries, row_start, block, 0)
        rotary_block = lax.dynamic_slice_in_dim(rotary, row_start, block, 0)
        query_pos = row_start + jnp.arange(block, dtype=jnp.int32)

        def key_step(index_key, state_now):
            running_max, running_sum, weighted = state_now
            key_start = (index_key * block).astype(jnp.int32)
            lat_piece = lax.dynamic_slice_in_dim(latent_wide, key_start, block, 1)
            rope_piece = lax.dynamic_slice_in_dim(rope_wide, key_start, block, 1)
            scores = (jnp.einsum('thc,cs->ths', query_block, lat_piece) + jnp.einsum('thr,rs->ths', rotary_block, rope_piece)) * score_scale
            key_pos = key_start + jnp.arange(block, dtype=jnp.int32)
            allowed = key_pos[None, None, :] <= query_pos[:, None, None]
            scores = jnp.where(allowed, scores, -1e+30)
            new_max = jnp.maximum(running_max, lax.optimization_barrier(jnp.max(scores, axis=2)))
            weights = jnp.where(allowed, jnp.exp(scores - new_max[:, :, None]), 0.0)
            rescale = jnp.exp(running_max - new_max)
            rounded = lax.optimization_barrier(weights.astype(jnp.bfloat16)).astype(jnp.float32)
            running_sum = running_sum * rescale + lax.optimization_barrier(jnp.sum(weights, axis=2))
            weighted = weighted * rescale[:, :, None] + jnp.einsum('ths,cs->thc', rounded, lat_piece)
            return (new_max, running_sum, weighted)
        initial = (jnp.full((block, HEADS), -1e+30, jnp.float32), jnp.zeros((block, HEADS), jnp.float32), jnp.zeros((block, HEADS, KVR), jnp.float32))
        final = lax.fori_loop(0, index_block + 1, key_step, initial)
        return (final[2] / final[1][:, :, None]).astype(jnp.bfloat16)
    result = lax.map(one_block, jnp.arange(blocks, dtype=jnp.int32))
    return result.reshape(SEQ, HEADS, KVR)

def expert_outputs(normed, expert_ids, w_gate, w_up, w_down):
    total_rows = SEQ * TOPK
    flat_ids = expert_ids.reshape(total_rows)
    slots = N_CTX * CAP

    def one_expert(expert):
        picked = jnp.nonzero(flat_ids == expert, size=slots, fill_value=total_rows)[0].astype(jnp.int32)
        rows = normed[jnp.minimum(picked, total_rows - 1) // TOPK]
        gate_part = jnp.dot(rows, w_gate[expert], preferred_element_type=jnp.float32)
        up_part = jnp.dot(rows, w_up[expert], preferred_element_type=jnp.float32)
        hidden = (jax.nn.silu(gate_part) * up_part).astype(jnp.bfloat16)
        values = jnp.dot(hidden, w_down[expert], preferred_element_type=jnp.float32).astype(jnp.bfloat16)
        return (picked, values)
    picked, values = lax.map(one_expert, jnp.arange(EXPERTS, dtype=jnp.int32))
    outputs = jnp.zeros((total_rows, D), jnp.bfloat16)
    outputs = outputs.at[picked.reshape(-1)].set(values.reshape(-1, D), mode='drop')
    return outputs.reshape(SEQ, TOPK, D)

def reference(hidden_in, q_latent, q_rotary, latent, k_rotary, w_value, w_output, ffn_gain, w_gate, w_up, w_down, expert_ids, gate_index, gate_table):
    head_latent = attention_rows(q_latent, q_rotary, latent, k_rotary)
    head_value = jnp.einsum('thc,hcv->thv', head_latent.astype(jnp.float32), w_value.astype(jnp.float32)).astype(jnp.bfloat16)
    attended = hidden_in.astype(jnp.float32) + jnp.dot(head_value.reshape(SEQ, HEADS * VD), w_output, preferred_element_type=jnp.float32)
    mean_square = lax.optimization_barrier(jnp.mean(attended * attended, axis=1, keepdims=True))
    normed = (attended * lax.rsqrt(mean_square + 1e-06) * ffn_gain[None, :]).astype(jnp.bfloat16)
    expert_out = expert_outputs(normed, expert_ids, w_gate, w_up, w_down)
    gate = gate_table[gate_index]
    mixed = attended + lax.optimization_barrier(jnp.sum(gate[:, :, None] * expert_out.astype(jnp.float32), axis=1))
    return mixed.astype(jnp.bfloat16)
```

```python
import functools
import math

import jax
import jax.numpy as jnp
from jax import lax
from jax.experimental import pallas as pl
from jax.experimental.pallas import tpu as pltpu
from jax.sharding import PartitionSpec as P

ROPE = 64
NOPE = 128

MESH = pl.DeviceIdType.MESH
DMA = pltpu.SemaphoreType.DMA


def neighbours():
    h = lax.axis_index("hd")
    return h + 1 - 2 * lax.rem(h, 2), h + 2 - 4 * (h // 2)


def remote(src, dst, send, recv, ctx, hd):
    return pltpu.make_async_remote_copy(
        src_ref=src,
        dst_ref=dst,
        send_sem=send,
        recv_sem=recv,
        device_id={"ctx": ctx, "hd": hd},
        device_id_type=MESH,
    )


def greet(n, hd_count):
    c, h = lax.axis_index("ctx"), lax.axis_index("hd")
    barrier = pltpu.get_barrier_semaphore()

    def over_ctx(i, _):
        peer = {"ctx": lax.rem(c + i, n), "hd": h}
        pl.semaphore_signal(barrier, inc=1, device_id=peer, device_id_type=MESH)
        return 0

    lax.fori_loop(1, n, over_ctx, 0)
    for i in range(1, hd_count):
        peer = {"ctx": c, "hd": lax.rem(h + i, hd_count)}
        pl.semaphore_signal(barrier, inc=1, device_id=peer, device_id_type=MESH)
    pl.semaphore_wait(barrier, n - 1 + hd_count - 1)


def mm(a, b):
    return jnp.dot(a, b, preferred_element_type=jnp.float32)


def mm_t(a, b):
    return lax.dot_general(a, b, (((1,), (1,)), ((), ())), preferred_element_type=jnp.float32)


def layer_kernel(
    n, chunks, model_width,
    q_latent, q_rotary, latent, k_rotary, gain, ids, gate_index, table,
    hidden_hbm, wv_hbm, wo_hbm, wg_hbm, wu_hbm, wd_hbm,
    out,
    hidden, wv, wo, wg, wu, wd,
    src, keys, queries, rotary, top, norm, acc,
    psend, ra, rb_send, rb_recv, att, outgoing, arrived,
    yown, ysend, yrecv, xsend, xrecv, back, returned,
    w_s, k1_s, k1_r, kr_s, k2_s, k2_r, k3_s, k3_r, k4_s, k4_r,
    ra_s, ra_r, rb_s, rb_r, d_s, d_r,
    f1_s, f1_r, f2_s, f2_r, f3_s, f3_r, y_s, y_r, x_s, x_r, b_s, b_r,
):
    c, h = lax.axis_index("ctx"), lax.axis_index("hd")
    core, across = neighbours()
    diagonal = core + across - h
    share = out.shape[1]
    cap = outgoing.shape[1]
    per = n // chunks
    hd_count = model_width // share
    f32 = jnp.float32

    def cols(g):
        return pl.ds(pl.multiple_of(g * share, share), share)

    heads = wv.shape[0]
    lat_width, tokens = latent.shape
    rope_width = k_rotary.shape[0]
    lat_part, rope_part = lat_width // hd_count, rope_width // hd_count
    score_scale = 1.0 / math.sqrt(NOPE + ROPE)

    for g in range(hd_count):
        src[g, :lat_part, :] = latent[g * lat_part : (g + 1) * lat_part, :]
        src[g, lat_part:, :] = k_rotary[g * rope_part : (g + 1) * rope_part, :]
    greet(n, hd_count)

    z, y = c // 2, lax.rem(c, 2)
    partner = c + 1 - 2 * y

    def to_column(k):
        return remote(src.at[h], keys.at[c, h], k1_s.at[k], k1_r.at[c], 2 * k + y, h)

    def to_partner():
        return remote(src.at[h], keys.at[c, h], k1_s.at[z], k1_r.at[c], partner, h)

    def relay(s):
        piece = keys.at[s, h]
        return remote(piece, piece, kr_s.at[s], k1_r.at[s], partner, h)

    def share_keys(s, quarter, send, recv, hd):
        piece = keys.at[s, quarter]
        return remote(piece, piece, send.at[s], recv.at[s], c, hd)

    def source_at(t):
        w = t - y
        column = (w >= 1) & (w <= z)
        depth = w - z * (w > z).astype(jnp.int32)
        other = 1 - column.astype(jnp.int32)
        return 2 * (z - depth) + y + other * (1 - 2 * y), column

    def start_keys(k, _):
        to_column(k).start()
        return 0

    @pl.when(y == 0)
    def _():
        to_partner().start()

    lax.fori_loop(z + 1, n // 2, start_keys, 0)
    loads = [
        pltpu.make_async_copy(a, b, w_s.at[k])
        for k, (a, b) in enumerate(
            [(wv_hbm, wv), (wo_hbm, wo), (hidden_hbm, hidden), (wg_hbm.at[0], wg),
             (wu_hbm.at[0], wu), (wd_hbm.at[0], wd)]
        )
    ]
    for load in loads:
        load.start()

    width = (n + 127) // 128 * 128
    lane = lax.broadcasted_iota(jnp.int32, (tokens, width), 1)
    below = (
        lax.broadcasted_iota(jnp.int32, (tokens, tokens), 0)
        > lax.broadcasted_iota(jnp.int32, (tokens, tokens), 1)
    ).astype(f32).astype(jnp.bfloat16)
    earlier = lane.astype(f32) * cap
    places, place_rows, gates = [], [], []

    def column(ref, k):
        line = ref[k : k + 1, :].astype(f32)
        return jnp.transpose(jnp.broadcast_to(line, (128, tokens)))[:, :1]

    entries = lax.broadcasted_iota(jnp.int32, (tokens, table.shape[1]), 1)
    for k in range(ids.shape[0]):
        member = (column(ids, k) == lane.astype(f32)).astype(f32)
        rank = mm(below, member.astype(jnp.bfloat16)) + earlier
        place = jnp.sum(member * rank, axis=1, keepdims=True)
        earlier = earlier + jnp.sum(member, axis=0, keepdims=True)
        places.append(place)
        place_rows.append(jnp.transpose(jnp.broadcast_to(place, (tokens, 128)))[:1, :])
        chosen = column(gate_index, k) == entries.astype(f32)
        gates.append(jnp.sum(jnp.where(chosen, table[...], 0.0), axis=1, keepdims=True))

    def rows_hit(e):
        slot = (lax.broadcasted_iota(jnp.int32, (cap, tokens), 0) + e * cap).astype(f32)
        hit = jnp.zeros((cap, tokens), f32)
        for row in place_rows:
            hit = hit + (slot == row).astype(f32)
        return hit.astype(jnp.bfloat16)

    for a in range(heads):
        here = slice(a * tokens, (a + 1) * tokens)
        queries[here, :] = q_latent[:, a * lat_width : (a + 1) * lat_width]
        rotary[here, :] = q_rotary[:, a * rope_width : (a + 1) * rope_width]

    def scores_of(lat, rope):
        return (mm(queries[...], lat) + mm(rotary[...], rope)) * score_scale

    lat = latent[...]
    scores = scores_of(lat, k_rotary[...])
    row = lax.broadcasted_iota(jnp.int32, (heads * tokens, tokens), 0)
    allowed = lax.broadcasted_iota(jnp.int32, scores.shape, 1) <= lax.rem(row, tokens)
    scores = jnp.where(allowed, scores, -1e30)
    peak = jnp.max(scores, axis=1, keepdims=True)
    weights = jnp.where(allowed, jnp.exp(scores - peak), 0.0)
    top[...] = peak
    norm[...] = jnp.sum(weights, axis=1, keepdims=True)
    acc[...] = mm_t(weights.astype(jnp.bfloat16), lat)

    def key_step(t, _):
        @pl.when(t <= c)
        def _():
            s, column = source_at(t)
            relay(s).wait_recv()

            @pl.when(column)
            def _():
                relay(s).start()

            share_keys(s, h, k3_s, k3_r, across).start()
            share_keys(s, h, k2_s, k2_r, core).start()

        @pl.when((t >= 2) & (t <= c + 1))
        def _():
            s, _ = source_at(t - 1)
            share_keys(s, across, k3_s, k3_r, across).wait_recv()
            share_keys(s, across, k4_s, k4_r, core).start()

        @pl.when(t >= 3)
        def _():
            i, _ = source_at(t - 2)
            share_keys(i, core, k2_s, k2_r, core).wait_recv()
            share_keys(i, diagonal, k4_s, k4_r, core).wait_recv()
            lat = keys[i, :, :lat_part, :].reshape(lat_width, tokens)
            rope = keys[i, :, lat_part:, :].reshape(rope_width, tokens)
            scores = scores_of(lat, rope)
            before = top[...]
            peak = jnp.maximum(before, jnp.max(scores, axis=1, keepdims=True))
            weights = jnp.exp(scores - peak)
            rescale = jnp.exp(before - peak)
            top[...] = peak
            norm[...] = norm[...] * rescale + jnp.sum(weights, axis=1, keepdims=True)
            acc[...] = acc[...] * rescale + mm_t(weights.astype(jnp.bfloat16), lat)

        return 0

    lax.fori_loop(1, c + 3, key_step, 0)
    head_latent = (acc[...] / norm[...]).astype(jnp.bfloat16)
    loads[0].wait()
    loads[1].wait()
    head_value = jnp.concatenate(
        [
            mm(head_latent[a * tokens : (a + 1) * tokens, :], wv[a]).astype(jnp.bfloat16)
            for a in range(heads)
        ],
        axis=1,
    )

    def to_core(k):
        return remote(psend.at[k], ra.at[k], ra_s.at[k], ra_r.at[k], c, core)

    def to_across():
        return remote(rb_send, rb_recv, rb_s.at[0], rb_r.at[0], c, across)

    psend[1] = mm(head_value, wo[:, cols(diagonal)]).astype(jnp.bfloat16)
    to_core(1).start()
    across_part = mm(head_value, wo[:, cols(across)])
    to_core(1).wait_recv()
    rb_send[...] = (across_part + ra[1].astype(f32)).astype(jnp.bfloat16)
    to_across().start()
    psend[0] = mm(head_value, wo[:, cols(core)]).astype(jnp.bfloat16)
    to_core(0).start()
    own_part = mm(head_value, wo[:, cols(h)])
    loads[2].wait()
    to_core(0).wait_recv()
    base = hidden[:, cols(h)].astype(f32) + (own_part + ra[0].astype(f32))
    to_across().wait_recv()
    attended = base + rb_recv[...].astype(f32)
    att[...] = attended
    scaled = (attended * gain[:, cols(h)]).astype(jnp.bfloat16)

    def dispatch(to):
        return remote(outgoing.at[to], arrived.at[h, c], d_s.at[to], d_r.at[c], to, h)

    def arrival(s):
        return remote(outgoing.at[s], arrived.at[h, s], d_s.at[s], d_r.at[s], s, h)

    def send_rows(i, _):
        to = lax.rem(c + i, n)
        outgoing[to] = mm(rows_hit(to), scaled).astype(jnp.bfloat16)
        dispatch(to).start()
        return 0

    lax.fori_loop(1, n, send_rows, 0)
    arrived[h, c] = mm(rows_hit(c), scaled).astype(jnp.bfloat16)

    def share_rows(j, g, send, recv, hd):
        part = arrived.at[g, pl.ds(j * per, per)]
        return remote(part, part, send.at[j], recv.at[j], c, hd)

    def y_core(j):
        return remote(ysend.at[j], yrecv.at[j], y_s.at[j], y_r.at[j], c, core)

    def y_across(j):
        return remote(xsend.at[j], xrecv.at[j], x_s.at[j], x_r.at[j], c, across)

    def give_back(s):
        return remote(back.at[s], returned.at[c], b_s.at[s], b_r.at[c], s, h)

    def come_home(e):
        return remote(back.at[e], returned.at[e], b_s.at[e], b_r.at[e], e, h)

    inverse_gain = 1.0 / gain[...]
    inverse_gain = inverse_gain * inverse_gain

    def step(t, _):
        @pl.when(t < chunks)
        def _():
            j = t

            def landed(k, _):
                i = j * per + k

                @pl.when(i != c)
                def _():
                    arrival(i).wait_recv()

                return 0

            lax.fori_loop(0, per, landed, 0)
            share_rows(j, h, f2_s, f2_r, across).start()
            share_rows(j, h, f1_s, f1_r, core).start()

        @pl.when((t >= 1) & (t < chunks + 1))
        def _():
            j = t - 1
            share_rows(j, across, f2_s, f2_r, across).wait_recv()
            share_rows(j, across, f3_s, f3_r, core).start()

        @pl.when((t >= 2) & (t < chunks + 2))
        def _():
            j = t - 2
            share_rows(j, core, f1_s, f1_r, core).wait_recv()
            share_rows(j, diagonal, f3_s, f3_r, core).wait_recv()
            gate_part = jnp.zeros((per * cap, wg.shape[0]), f32)
            up_part = jnp.zeros((per * cap, wg.shape[0]), f32)
            squares = jnp.zeros((per * cap, share), f32)
            for g in range(hd_count):
                here = slice(g * share, (g + 1) * share)
                rows = arrived[g, pl.ds(j * per, per)].reshape(per * cap, share)
                wide = rows.astype(f32)
                squares = squares + wide * wide * inverse_gain[:, here]
                gate_part = gate_part + mm_t(rows, wg[:, g * share : (g + 1) * share])
                up_part = up_part + mm_t(rows, wu[:, g * share : (g + 1) * share])
            mean = jnp.sum(squares, axis=1, keepdims=True) / model_width
            inverse = lax.rsqrt(mean + 1e-06)
            gate_part = gate_part * inverse
            up_part = up_part * inverse
            units = (gate_part / (1.0 + jnp.exp(-gate_part)) * up_part).astype(jnp.bfloat16)
            ysend[j, 0] = mm(units, wd[:, cols(core)]).astype(jnp.bfloat16)
            ysend[j, 1] = mm(units, wd[:, cols(diagonal)]).astype(jnp.bfloat16)
            y_core(j).start()
            yown[j, 0] = mm(units, wd[:, cols(h)])
            yown[j, 1] = mm(units, wd[:, cols(across)])

        @pl.when((t >= 3) & (t < chunks + 3))
        def _():
            j = t - 3
            y_core(j).wait_recv()
            xsend[j] = (yown[j, 1] + yrecv[j, 1].astype(f32)).astype(jnp.bfloat16)
            y_across(j).start()

        @pl.when(t >= 4)
        def _():
            j = t - 4
            y_across(j).wait_recv()
            whole = yown[j, 0] + yrecv[j, 0].astype(f32) + xrecv[j].astype(f32)
            back[pl.ds(j * per, per)] = whole.astype(jnp.bfloat16).reshape(per, cap, share)

            def go(k, _):
                i = j * per + k

                @pl.when(i != c)
                def _():
                    give_back(i).start()

                return 0

            lax.fori_loop(0, per, go, 0)

        return 0

    for load in loads[3:]:
        load.wait()
    lax.fori_loop(0, chunks + 4, step, 0)
    returned[c] = back[c]

    def home(i, _):
        come_home(lax.rem(c + i, n)).wait_recv()
        return 0

    lax.fori_loop(1, n, home, 0)
    rows = returned[...].reshape(n * cap, share)
    mixed = att[...]
    slot = lax.broadcasted_iota(jnp.int32, (tokens, n * cap), 1).astype(f32)
    for place, gate in zip(places, gates):
        mixed = mixed + gate * mm((slot == place).astype(f32).astype(jnp.bfloat16), rows)
    out[...] = mixed.astype(out.dtype)

    def sent_keys(k, _):
        to_column(k).wait_send()
        return 0

    def sent_relays(k, _):
        relay(2 * k + y).wait_send()
        return 0

    def sent_shares(i, _):
        share_keys(i, h, k2_s, k2_r, core).wait_send()
        share_keys(i, h, k3_s, k3_r, across).wait_send()
        share_keys(i, across, k4_s, k4_r, core).wait_send()
        return 0

    @pl.when(y == 0)
    def _():
        to_partner().wait_send()

    lax.fori_loop(z + 1, n // 2, sent_keys, 0)
    lax.fori_loop(0, z, sent_relays, 0)
    lax.fori_loop(0, c, sent_shares, 0)
    to_core(0).wait_send()
    to_core(1).wait_send()
    to_across().wait_send()

    def sent(i, _):
        to = lax.rem(c + i, n)
        dispatch(to).wait_send()
        give_back(to).wait_send()
        return 0

    lax.fori_loop(1, n, sent, 0)

    def sent_chunk(j, _):
        share_rows(j, h, f1_s, f1_r, core).wait_send()
        share_rows(j, h, f2_s, f2_r, across).wait_send()
        share_rows(j, across, f3_s, f3_r, core).wait_send()
        y_core(j).wait_send()
        y_across(j).wait_send()
        return 0

    lax.fori_loop(0, chunks, sent_chunk, 0)


def on_device(
    hidden_in,
    q_latent,
    q_rotary,
    latent,
    k_rotary,
    w_value,
    w_output,
    ffn_gain,
    w_gate,
    w_up,
    w_down,
    expert_ids,
    gate_index,
    gate_table,
):
    n, hd_count = lax.axis_size("ctx"), lax.axis_size("hd")
    tokens, width = hidden_in.shape
    share = width // hd_count
    needed = 3 * tokens * expert_ids.shape[1] // (2 * n * w_gate.shape[0])
    cap = (needed + 15) // 16 * 16
    chunks = math.gcd(n, 8)
    rows = n // chunks * cap
    bf = jnp.bfloat16
    f32 = jnp.float32
    vm = pltpu.VMEM
    lat_width, rope_width = latent.shape[0], k_rotary.shape[0]
    stacked = w_value.shape[0] * tokens
    quarter = (lat_width + rope_width) // hd_count
    return pl.pallas_call(
        functools.partial(layer_kernel, n, chunks, width),
        out_shape=jax.ShapeDtypeStruct((tokens, share), bf),
        in_specs=[pl.BlockSpec(memory_space=pltpu.VMEM)] * 8
        + [pl.BlockSpec(memory_space=pl.ANY)] * 6,
        out_specs=pl.BlockSpec(memory_space=pltpu.VMEM),
        scratch_shapes=[
            vm(hidden_in.shape, bf),
            vm(w_value.shape, bf),
            vm(w_output.shape, bf),
            vm(w_gate.shape[:0:-1], bf),
            vm(w_up.shape[:0:-1], bf),
            vm(w_down.shape[1:], bf),
            vm((hd_count, quarter, tokens), bf),
            vm((n, hd_count, quarter, tokens), bf),
            vm((stacked, lat_width), bf),
            vm((stacked, rope_width), bf),
            vm((stacked, 1), f32),
            vm((stacked, 1), f32),
            vm((stacked, lat_width), f32),
            vm((2, tokens, share), bf),
            vm((2, tokens, share), bf),
            vm((tokens, share), bf),
            vm((tokens, share), bf),
            vm((tokens, share), f32),
            vm((n, cap, share), bf),
            vm((hd_count, n, cap, share), bf),
            vm((chunks, 2, rows, share), f32),
            vm((chunks, 2, rows, share), bf),
            vm((chunks, 2, rows, share), bf),
            vm((chunks, rows, share), bf),
            vm((chunks, rows, share), bf),
            vm((n, cap, share), bf),
            vm((n, cap, share), bf),
        ]
        + [DMA((6,))]
        + [DMA((n,))] * 9
        + [DMA((2,))] * 2
        + [DMA((1,))] * 2
        + [DMA((n,))] * 2
        + [DMA((chunks,))] * 10
        + [DMA((n,))] * 2,
        compiler_params=pltpu.CompilerParams(
            collective_id=0, has_side_effects=True, vmem_limit_bytes=60 * 1024 * 1024
        ),
    )(
        q_latent,
        q_rotary,
        latent,
        k_rotary,
        ffn_gain[None, :],
        expert_ids.T,
        gate_index.T,
        gate_table[None, :],
        hidden_in,
        w_value,
        w_output,
        jnp.swapaxes(w_gate, 1, 2),
        jnp.swapaxes(w_up, 1, 2),
        w_down,
    )


def solution(mesh):
    in_specs = (
        P("ctx", None),
        P("ctx", "hd"),
        P("ctx", "hd"),
        P(None, "ctx"),
        P(None, "ctx"),
        P("hd", None, None),
        P("hd", None),
        P(),
        P("ctx", None, "hd"),
        P("ctx", None, "hd"),
        P("ctx", "hd", None),
        P("ctx", None),
        P("ctx", None),
        P(),
    )
    out_specs = P("ctx", "hd")
    return jax.shard_map(
        on_device, mesh=mesh, in_specs=in_specs, out_specs=out_specs, check_vma=False
    )
```

```python
import functools
import math

import jax
import jax.numpy as jnp
from jax import lax
from jax.experimental import pallas as pl
from jax.experimental.pallas import tpu as pltpu
from jax.sharding import PartitionSpec as P

ROPE = 64
NOPE = 128

MESH = pl.DeviceIdType.MESH
DMA = pltpu.SemaphoreType.DMA


def neighbours():
    h = lax.axis_index("hd")
    return h + 1 - 2 * lax.rem(h, 2), h + 2 - 4 * (h // 2)


def remote(src, dst, send, recv, ctx, hd):
    return pltpu.make_async_remote_copy(
        src_ref=src,
        dst_ref=dst,
        send_sem=send,
        recv_sem=recv,
        device_id={"ctx": ctx, "hd": hd},
        device_id_type=MESH,
    )


def greet(n, hd_count):
    c, h = lax.axis_index("ctx"), lax.axis_index("hd")
    barrier = pltpu.get_barrier_semaphore()

    def over_ctx(i, _):
        peer = {"ctx": lax.rem(c + i, n), "hd": h}
        pl.semaphore_signal(barrier, inc=1, device_id=peer, device_id_type=MESH)
        return 0

    lax.fori_loop(1, n, over_ctx, 0)
    for i in range(1, hd_count):
        peer = {"ctx": c, "hd": lax.rem(h + i, hd_count)}
        pl.semaphore_signal(barrier, inc=1, device_id=peer, device_id_type=MESH)
    peer = {"ctx": c + 1 - 2 * lax.rem(c, 2), "hd": neighbours()[1]}
    pl.semaphore_signal(barrier, inc=1, device_id=peer, device_id_type=MESH)
    pl.semaphore_wait(barrier, n + hd_count - 1)


def mm(a, b):
    return jnp.dot(a, b, preferred_element_type=jnp.float32)


def mm_t(a, b):
    return lax.dot_general(a, b, (((1,), (1,)), ((), ())), preferred_element_type=jnp.float32)


def layer_kernel(
    n, chunks, model_width,
    q_latent, q_rotary, latent, k_rotary, gain, ids, gate_index, table,
    hidden_hbm, wv_hbm, wo_hbm, wg_hbm, wu_hbm, wd_hbm,
    out,
    hidden, wv, wo, wg, wu, wd,
    src, keys, queries, rotary, top, norm, acc, hits, picks, gate_of,
    psend, ra, rb_send, rb_recv, att, outgoing, arrived,
    yown, ysend, yrecv, xsend, xrecv, back, returned,
    w_s, kw_s, k1_s, k1_r, kr_s, kx_s, k2_s, k2_r, k3_s, k3_r, k4_s, k4_r,
    ra_s, ra_r, rb_s, rb_r, d_s, d_r,
    f1_s, f1_r, f2_s, f2_r, f3_s, f3_r, y_s, y_r, x_s, x_r, b_s, b_r,
):
    c, h = lax.axis_index("ctx"), lax.axis_index("hd")
    core, across = neighbours()
    diagonal = core + across - h
    share = out.shape[1]
    cap = outgoing.shape[1]
    per = n // chunks
    hd_count = model_width // share
    f32 = jnp.float32

    def cols(g):
        return pl.ds(pl.multiple_of(g * share, share), share)

    heads = wv.shape[0]
    lat_width, tokens = latent.shape
    rope_width = k_rotary.shape[0]
    lat_part, rope_part = lat_width // hd_count, rope_width // hd_count
    score_scale = 1.0 / math.sqrt(NOPE + ROPE)

    loads = [
        pltpu.make_async_copy(a, b, w_s.at[k])
        for k, (a, b) in enumerate(
            [(wv_hbm, wv), (wo_hbm, wo), (hidden_hbm, hidden), (wg_hbm.at[0], wg),
             (wu_hbm.at[0], wu), (wd_hbm.at[0], wd)]
        )
    ]
    for load in loads:
        load.start()

    for g in range(hd_count):
        src[g, :lat_part, :] = latent[g * lat_part : (g + 1) * lat_part, :]
        src[g, lat_part:, :] = k_rotary[g * rope_part : (g + 1) * rope_part, :]
    greet(n, hd_count)

    z, y = c // 2, lax.rem(c, 2)
    partner = c + 1 - 2 * y

    def to_column(k):
        return remote(src.at[h], keys.at[c, h], k1_s.at[k], k1_r.at[c], 2 * k + y, h)

    def to_partner():
        return remote(src.at[h], keys.at[c, h], k1_s.at[z], k1_r.at[c], partner, h)

    def second_to_partner():
        return remote(src.at[across], keys.at[c, across], kw_s.at[0], k3_r.at[c], partner, h)

    def relay(s):
        piece = keys.at[s, h]
        return remote(piece, piece, kr_s.at[s], k1_r.at[s], partner, h)

    def relay_across(s):
        piece = keys.at[s, h]
        return remote(piece, piece, kx_s.at[s], k3_r.at[s], partner, across)

    def share_keys(s, quarter, send, recv, hd):
        piece = keys.at[s, quarter]
        return remote(piece, piece, send.at[s], recv.at[s], c, hd)

    def source_at(t):
        w = t - y
        column = (w >= 1) & (w <= z)
        depth = w - z * (w > z).astype(jnp.int32)
        other = 1 - column.astype(jnp.int32)
        return 2 * (z - depth) + y + other * (1 - 2 * y), column

    def start_keys(k, _):
        to_column(k).start()
        return 0

    @pl.when(y == 0)
    def _():
        to_partner().start()
        second_to_partner().start()

    lax.fori_loop(z + 1, n // 2, start_keys, 0)
    width = (n + 127) // 128 * 128
    lane = lax.broadcasted_iota(jnp.int32, (tokens, width), 1)
    below = (
        lax.broadcasted_iota(jnp.int32, (tokens, tokens), 0)
        > lax.broadcasted_iota(jnp.int32, (tokens, tokens), 1)
    ).astype(f32).astype(jnp.bfloat16)
    earlier = lane.astype(f32) * cap
    places, place_rows, gates = [], [], []

    def column(ref, k):
        line = ref[k : k + 1, :].astype(f32)
        return jnp.transpose(jnp.broadcast_to(line, (128, tokens)))[:, :1]

    entries = lax.broadcasted_iota(jnp.int32, (tokens, table.shape[1]), 1)
    for k in range(ids.shape[0]):
        member = (column(ids, k) == lane.astype(f32)).astype(f32)
        rank = mm(below, member.astype(jnp.bfloat16)) + earlier
        place = jnp.sum(member * rank, axis=1, keepdims=True)
        earlier = earlier + jnp.sum(member, axis=0, keepdims=True)
        places.append(place)
        place_rows.append(jnp.transpose(jnp.broadcast_to(place, (tokens, 128)))[:1, :])
        chosen = column(gate_index, k) == entries.astype(f32)
        gates.append(jnp.sum(jnp.where(chosen, table[...], 0.0), axis=1, keepdims=True))

    def find_rows(e, _):
        slot = (lax.broadcasted_iota(jnp.int32, (cap, tokens), 0) + e * cap).astype(f32)
        hit = jnp.zeros((cap, tokens), f32)
        for row in place_rows:
            hit = hit + (slot == row).astype(f32)
        hits[pl.ds(pl.multiple_of(e * cap, cap), cap), :] = hit.astype(jnp.bfloat16)
        return 0

    lax.fori_loop(0, n, find_rows, 0)
    slot = lax.broadcasted_iota(jnp.int32, (tokens, n * cap), 1).astype(f32)
    for k, place in enumerate(places):
        picks[k] = (slot == place).astype(f32).astype(jnp.bfloat16)
        gate_of[k] = gates[k]

    for a in range(heads):
        here = slice(a * tokens, (a + 1) * tokens)
        queries[here, :] = q_latent[:, a * lat_width : (a + 1) * lat_width]
        rotary[here, :] = q_rotary[:, a * rope_width : (a + 1) * rope_width]

    def scores_of(lat, rope):
        return (mm(queries[...], lat) + mm(rotary[...], rope)) * score_scale

    lat = latent[...]
    scores = scores_of(lat, k_rotary[...])
    row = lax.broadcasted_iota(jnp.int32, (heads * tokens, tokens), 0)
    allowed = lax.broadcasted_iota(jnp.int32, scores.shape, 1) <= lax.rem(row, tokens)
    scores = jnp.where(allowed, scores, -1e30)
    peak = jnp.max(scores, axis=1, keepdims=True)
    weights = jnp.where(allowed, jnp.exp(scores - peak), 0.0)
    top[...] = peak
    norm[...] = jnp.sum(weights, axis=1, keepdims=True)
    acc[...] = mm_t(weights.astype(jnp.bfloat16), lat)

    second, third = 2, 4

    def key_step(t, _):
        @pl.when(t <= c)
        def _():
            s, column = source_at(t)
            relay(s).wait_recv()

            @pl.when(column)
            def _():
                relay(s).start()
                relay_across(s).start()
                share_keys(s, h, k3_s, k3_r, across).start()

            share_keys(s, h, k2_s, k2_r, core).start()

        @pl.when((t > second) & (t <= c + second))
        def _():
            s, _ = source_at(t - second)
            share_keys(s, across, k3_s, k3_r, across).wait_recv()
            share_keys(s, across, k4_s, k4_r, core).start()

        @pl.when(t > third)
        def _():
            i, _ = source_at(t - third)
            share_keys(i, core, k2_s, k2_r, core).wait_recv()
            share_keys(i, diagonal, k4_s, k4_r, core).wait_recv()
            lat = keys[i, :, :lat_part, :].reshape(lat_width, tokens)
            rope = keys[i, :, lat_part:, :].reshape(rope_width, tokens)
            scores = scores_of(lat, rope)
            before = top[...]
            peak = jnp.maximum(before, jnp.max(scores, axis=1, keepdims=True))
            weights = jnp.exp(scores - peak)
            rescale = jnp.exp(before - peak)
            top[...] = peak
            norm[...] = norm[...] * rescale + jnp.sum(weights, axis=1, keepdims=True)
            acc[...] = acc[...] * rescale + mm_t(weights.astype(jnp.bfloat16), lat)

        return 0

    lax.fori_loop(1, c + 1 + third, key_step, 0)
    head_latent = (acc[...] / norm[...]).astype(jnp.bfloat16)
    loads[0].wait()
    loads[1].wait()
    head_value = jnp.concatenate(
        [
            mm(head_latent[a * tokens : (a + 1) * tokens, :], wv[a]).astype(jnp.bfloat16)
            for a in range(heads)
        ],
        axis=1,
    )

    def to_core(k):
        return remote(psend.at[k], ra.at[k], ra_s.at[k], ra_r.at[k], c, core)

    def to_across():
        return remote(rb_send, rb_recv, rb_s.at[0], rb_r.at[0], c, across)

    def dispatch(to):
        return remote(outgoing.at[to], arrived.at[h, c], d_s.at[to], d_r.at[c], to, h)

    def arrival(s):
        return remote(outgoing.at[s], arrived.at[h, s], d_s.at[s], d_r.at[s], s, h)

    def share_rows(j, g, send, recv, hd):
        part = arrived.at[g, pl.ds(j * per, per)]
        return remote(part, part, send.at[j], recv.at[j], c, hd)

    def take_chunk(j):
        def landed(k, _):
            i = j * per + k

            @pl.when(i != c)
            def _():
                arrival(i).wait_recv()

            return 0

        lax.fori_loop(0, per, landed, 0)
        share_rows(j, h, f2_s, f2_r, across).start()
        share_rows(j, h, f1_s, f1_r, core).start()

    def pass_chunk(j):
        share_rows(j, across, f2_s, f2_r, across).wait_recv()
        share_rows(j, across, f3_s, f3_r, core).start()

    late = c // per >= chunks - 2
    lead = 2 * late.astype(jnp.int32)

    psend[1] = mm(head_value, wo[:, cols(diagonal)]).astype(jnp.bfloat16)
    to_core(1).start()
    across_part = mm(head_value, wo[:, cols(across)])
    to_core(1).wait_recv()
    rb_send[...] = (across_part + ra[1].astype(f32)).astype(jnp.bfloat16)
    to_across().start()
    psend[0] = mm(head_value, wo[:, cols(core)]).astype(jnp.bfloat16)
    to_core(0).start()
    own_part = mm(head_value, wo[:, cols(h)])
    loads[2].wait()
    to_core(0).wait_recv()
    base = hidden[:, cols(h)].astype(f32) + (own_part + ra[0].astype(f32))

    @pl.when(late)
    def _():
        take_chunk(0)
        take_chunk(1)

    to_across().wait_recv()
    attended = base + rb_recv[...].astype(f32)
    att[...] = attended
    scaled = (attended * gain[:, cols(h)]).astype(jnp.bfloat16)

    outgoing[...] = mm(hits[...], scaled).astype(jnp.bfloat16).reshape(n, cap, share)

    def send_rows(i, _):
        dispatch(lax.rem(c + i, n)).start()
        return 0

    lax.fori_loop(1, n, send_rows, 0)
    arrived[h, c] = outgoing[c]

    def y_core(j):
        return remote(ysend.at[j], yrecv.at[j], y_s.at[j], y_r.at[j], c, core)

    def y_across(j):
        return remote(xsend.at[j], xrecv.at[j], x_s.at[j], x_r.at[j], c, across)

    def give_back(s):
        return remote(back.at[s], returned.at[c], b_s.at[s], b_r.at[c], s, h)

    def come_home(e):
        return remote(back.at[e], returned.at[e], b_s.at[e], b_r.at[e], e, h)

    inverse_gain = 1.0 / gain[...]
    inverse_gain = inverse_gain * inverse_gain

    def step(t, _):
        @pl.when((t + 2 >= lead) & (t + 2 < chunks))
        def _():
            take_chunk(t + 2)

        @pl.when((t >= 0) & (t + 1 < chunks) | (t == -1))
        def _():
            pass_chunk(t + 1)

        @pl.when((t >= 0) & (t < chunks))
        def _():
            j = t
            share_rows(j, core, f1_s, f1_r, core).wait_recv()
            share_rows(j, diagonal, f3_s, f3_r, core).wait_recv()
            gate_part = jnp.zeros((per * cap, wg.shape[0]), f32)
            up_part = jnp.zeros((per * cap, wg.shape[0]), f32)
            squares = jnp.zeros((per * cap, share), f32)
            for g in range(hd_count):
                here = slice(g * share, (g + 1) * share)
                rows = arrived[g, pl.ds(j * per, per)].reshape(per * cap, share)
                wide = rows.astype(f32)
                squares = squares + wide * wide * inverse_gain[:, here]
                gate_part = gate_part + mm_t(rows, wg[:, g * share : (g + 1) * share])
                up_part = up_part + mm_t(rows, wu[:, g * share : (g + 1) * share])
            mean = jnp.sum(squares, axis=1, keepdims=True) / model_width
            inverse = lax.rsqrt(mean + 1e-06)
            gate_part = gate_part * inverse
            up_part = up_part * inverse
            units = (gate_part / (1.0 + jnp.exp(-gate_part)) * up_part).astype(jnp.bfloat16)
            ysend[j, 0] = mm(units, wd[:, cols(core)]).astype(jnp.bfloat16)
            ysend[j, 1] = mm(units, wd[:, cols(diagonal)]).astype(jnp.bfloat16)
            y_core(j).start()
            yown[j, 0] = mm(units, wd[:, cols(h)])
            yown[j, 1] = mm(units, wd[:, cols(across)])

        @pl.when((t >= 1) & (t < chunks + 1))
        def _():
            j = t - 1
            y_core(j).wait_recv()
            xsend[j] = (yown[j, 1] + yrecv[j, 1].astype(f32)).astype(jnp.bfloat16)
            y_across(j).start()

        @pl.when(t >= 2)
        def _():
            j = t - 2
            y_across(j).wait_recv()
            whole = yown[j, 0] + yrecv[j, 0].astype(f32) + xrecv[j].astype(f32)
            back[pl.ds(j * per, per)] = whole.astype(jnp.bfloat16).reshape(per, cap, share)

            def go(k, _):
                i = j * per + k

                @pl.when(i != c)
                def _():
                    give_back(i).start()

                return 0

            lax.fori_loop(0, per, go, 0)

        return 0

    for load in loads[3:]:
        load.wait()
    lax.fori_loop(-2, chunks + 2, step, 0)
    returned[c] = back[c]

    def home(i, _):
        come_home(lax.rem(c + i, n)).wait_recv()
        return 0

    lax.fori_loop(1, n, home, 0)
    rows = returned[...].reshape(n * cap, share)
    mixed = att[...]
    for k in range(len(places)):
        mixed = mixed + gate_of[k] * mm(picks[k], rows)
    out[...] = mixed.astype(out.dtype)

    def sent_keys(k, _):
        to_column(k).wait_send()
        return 0

    def sent_relays(k, _):
        s = 2 * k + y
        relay(s).wait_send()
        relay_across(s).wait_send()
        share_keys(s, h, k3_s, k3_r, across).wait_send()
        return 0

    def sent_shares(i, _):
        share_keys(i, h, k2_s, k2_r, core).wait_send()
        share_keys(i, across, k4_s, k4_r, core).wait_send()
        return 0

    @pl.when(y == 0)
    def _():
        to_partner().wait_send()
        second_to_partner().wait_send()

    lax.fori_loop(z + 1, n // 2, sent_keys, 0)
    lax.fori_loop(0, z, sent_relays, 0)
    lax.fori_loop(0, c, sent_shares, 0)
    to_core(0).wait_send()
    to_core(1).wait_send()
    to_across().wait_send()

    def sent(i, _):
        to = lax.rem(c + i, n)
        dispatch(to).wait_send()
        give_back(to).wait_send()
        return 0

    lax.fori_loop(1, n, sent, 0)

    def sent_chunk(j, _):
        share_rows(j, h, f1_s, f1_r, core).wait_send()
        share_rows(j, h, f2_s, f2_r, across).wait_send()
        share_rows(j, across, f3_s, f3_r, core).wait_send()
        y_core(j).wait_send()
        y_across(j).wait_send()
        return 0

    lax.fori_loop(0, chunks, sent_chunk, 0)


def on_device(
    hidden_in,
    q_latent,
    q_rotary,
    latent,
    k_rotary,
    w_value,
    w_output,
    ffn_gain,
    w_gate,
    w_up,
    w_down,
    expert_ids,
    gate_index,
    gate_table,
):
    n, hd_count = lax.axis_size("ctx"), lax.axis_size("hd")
    tokens, width = hidden_in.shape
    share = width // hd_count
    needed = 3 * tokens * expert_ids.shape[1] // (2 * n * w_gate.shape[0])
    cap = (needed + 15) // 16 * 16
    chunks = math.gcd(n, 8)
    rows = n // chunks * cap
    bf = jnp.bfloat16
    f32 = jnp.float32
    vm = pltpu.VMEM
    lat_width, rope_width = latent.shape[0], k_rotary.shape[0]
    stacked = w_value.shape[0] * tokens
    quarter = (lat_width + rope_width) // hd_count
    return pl.pallas_call(
        functools.partial(layer_kernel, n, chunks, width),
        out_shape=jax.ShapeDtypeStruct((tokens, share), bf),
        in_specs=[pl.BlockSpec(memory_space=pltpu.VMEM)] * 8
        + [pl.BlockSpec(memory_space=pl.ANY)] * 6,
        out_specs=pl.BlockSpec(memory_space=pltpu.VMEM),
        scratch_shapes=[
            vm(hidden_in.shape, bf),
            vm(w_value.shape, bf),
            vm(w_output.shape, bf),
            vm(w_gate.shape[:0:-1], bf),
            vm(w_up.shape[:0:-1], bf),
            vm(w_down.shape[1:], bf),
            vm((hd_count, quarter, tokens), bf),
            vm((n, hd_count, quarter, tokens), bf),
            vm((stacked, lat_width), bf),
            vm((stacked, rope_width), bf),
            vm((stacked, 1), f32),
            vm((stacked, 1), f32),
            vm((stacked, lat_width), f32),
            vm((n * cap, tokens), bf),
            vm((expert_ids.shape[1], tokens, n * cap), bf),
            vm((expert_ids.shape[1], tokens, 1), f32),
            vm((2, tokens, share), bf),
            vm((2, tokens, share), bf),
            vm((tokens, share), bf),
            vm((tokens, share), bf),
            vm((tokens, share), f32),
            vm((n, cap, share), bf),
            vm((hd_count, n, cap, share), bf),
            vm((chunks, 2, rows, share), f32),
            vm((chunks, 2, rows, share), bf),
            vm((chunks, 2, rows, share), bf),
            vm((chunks, rows, share), bf),
            vm((chunks, rows, share), bf),
            vm((n, cap, share), bf),
            vm((n, cap, share), bf),
        ]
        + [DMA((6,)), DMA((1,))]
        + [DMA((n,))] * 10
        + [DMA((2,))] * 2
        + [DMA((1,))] * 2
        + [DMA((n,))] * 2
        + [DMA((chunks,))] * 10
        + [DMA((n,))] * 2,
        compiler_params=pltpu.CompilerParams(
            collective_id=0, has_side_effects=True, vmem_limit_bytes=60 * 1024 * 1024
        ),
    )(
        q_latent,
        q_rotary,
        latent,
        k_rotary,
        ffn_gain[None, :],
        expert_ids.T,
        gate_index.T,
        gate_table[None, :],
        hidden_in,
        w_value,
        w_output,
        jnp.swapaxes(w_gate, 1, 2),
        jnp.swapaxes(w_up, 1, 2),
        w_down,
    )


def solution(mesh):
    in_specs = (
        P("ctx", None),
        P("ctx", "hd"),
        P("ctx", "hd"),
        P(None, "ctx"),
        P(None, "ctx"),
        P("hd", None, None),
        P("hd", None),
        P(),
        P("ctx", None, "hd"),
        P("ctx", None, "hd"),
        P("ctx", "hd", None),
        P("ctx", None),
        P("ctx", None),
        P(),
    )
    out_specs = P("ctx", "hd")
    return jax.shard_map(
        on_device, mesh=mesh, in_specs=in_specs, out_specs=out_specs, check_vma=False
    )
```

```python
import functools
import math

import jax
import jax.numpy as jnp
from jax import lax
from jax.experimental import pallas as pl
from jax.experimental.pallas import tpu as pltpu
from jax.sharding import PartitionSpec as P

ROPE = 64
NOPE = 128

MESH = pl.DeviceIdType.MESH
DMA = pltpu.SemaphoreType.DMA


def neighbours():
    h = lax.axis_index("hd")
    return h + 1 - 2 * lax.rem(h, 2), h + 2 - 4 * (h // 2)


def remote(src, dst, send, recv, ctx, hd):
    return pltpu.make_async_remote_copy(
        src_ref=src,
        dst_ref=dst,
        send_sem=send,
        recv_sem=recv,
        device_id={"ctx": ctx, "hd": hd},
        device_id_type=MESH,
    )


def greet(n, hd_count):
    c, h = lax.axis_index("ctx"), lax.axis_index("hd")
    barrier = pltpu.get_barrier_semaphore()

    def over_ctx(i, _):
        peer = {"ctx": lax.rem(c + i, n), "hd": h}
        pl.semaphore_signal(barrier, inc=1, device_id=peer, device_id_type=MESH)
        return 0

    lax.fori_loop(1, n, over_ctx, 0)
    for i in range(1, hd_count):
        peer = {"ctx": c, "hd": lax.rem(h + i, hd_count)}
        pl.semaphore_signal(barrier, inc=1, device_id=peer, device_id_type=MESH)
    peer = {"ctx": c + 1 - 2 * lax.rem(c, 2), "hd": neighbours()[1]}
    pl.semaphore_signal(barrier, inc=1, device_id=peer, device_id_type=MESH)
    pl.semaphore_wait(barrier, n + hd_count - 1)


def mm(a, b):
    return jnp.dot(a, b, preferred_element_type=jnp.float32)


def mm_t(a, b):
    return lax.dot_general(a, b, (((1,), (1,)), ((), ())), preferred_element_type=jnp.float32)


def layer_kernel(
    n, chunks, model_width,
    q_latent, q_rotary, latent, k_rotary, gain, ids, gate_index, table,
    hidden_hbm, wv_hbm, wo_hbm, wg_hbm, wu_hbm, wd_hbm,
    out,
    hidden, wv, wo, wg, wu, wd,
    src, keys, queries, rotary, top, norm, acc, hits, picks, gate_of,
    psend, ra, rb_send, rb_recv, att, outgoing, arrived,
    yown, ysend, yrecv, xsend, xrecv, back, returned,
    w_s, kw_s, k1_s, k1_r, kr_s, kx_s, k2_s, k2_r, k3_s, k3_r, k4_s, k4_r,
    ra_s, ra_r, rb_s, rb_r, d_s, d_r,
    f1_s, f1_r, f2_s, f2_r, f3_s, f3_r, y_s, y_r, x_s, x_r, b_s, b_r,
):
    c, h = lax.axis_index("ctx"), lax.axis_index("hd")
    core, across = neighbours()
    diagonal = core + across - h
    share = out.shape[1]
    cap = outgoing.shape[1]
    per = n // chunks
    hd_count = model_width // share
    f32 = jnp.float32

    def cols(g):
        return pl.ds(pl.multiple_of(g * share, share), share)

    heads = wv.shape[0]
    lat_width, tokens = latent.shape
    rope_width = k_rotary.shape[0]
    lat_part, rope_part = lat_width // hd_count, rope_width // hd_count
    score_scale = 1.0 / math.sqrt(NOPE + ROPE)

    loads = [
        pltpu.make_async_copy(a, b, w_s.at[k])
        for k, (a, b) in enumerate(
            [(wv_hbm, wv), (wo_hbm, wo), (hidden_hbm, hidden), (wg_hbm.at[0], wg),
             (wu_hbm.at[0], wu), (wd_hbm.at[0], wd)]
        )
    ]
    for load in loads:
        load.start()

    for g in range(hd_count):
        src[g, :lat_part, :] = latent[g * lat_part : (g + 1) * lat_part, :]
        src[g, lat_part:, :] = k_rotary[g * rope_part : (g + 1) * rope_part, :]
    greet(n, hd_count)

    z, y = c // 2, lax.rem(c, 2)
    partner = c + 1 - 2 * y

    def to_column(k):
        return remote(src.at[h], keys.at[c, h], k1_s.at[k], k1_r.at[c], 2 * k + y, h)

    def to_partner():
        return remote(src.at[h], keys.at[c, h], k1_s.at[z], k1_r.at[c], partner, h)

    def second_to_partner():
        return remote(src.at[across], keys.at[c, across], kw_s.at[0], k3_r.at[c], partner, h)

    def relay(s):
        piece = keys.at[s, h]
        return remote(piece, piece, kr_s.at[s], k1_r.at[s], partner, h)

    def relay_across(s):
        piece = keys.at[s, h]
        return remote(piece, piece, kx_s.at[s], k3_r.at[s], partner, across)

    def share_keys(s, quarter, send, recv, hd):
        piece = keys.at[s, quarter]
        return remote(piece, piece, send.at[s], recv.at[s], c, hd)

    def source_at(t):
        w = t - y
        column = (w >= 1) & (w <= z)
        depth = w - z * (w > z).astype(jnp.int32)
        other = 1 - column.astype(jnp.int32)
        return 2 * (z - depth) + y + other * (1 - 2 * y), column

    def start_keys(k, _):
        to_column(k).start()
        return 0

    @pl.when(y == 0)
    def _():
        to_partner().start()
        second_to_partner().start()

    lax.fori_loop(z + 1, n // 2, start_keys, 0)
    width = (n + 127) // 128 * 128
    lane = lax.broadcasted_iota(jnp.int32, (tokens, width), 1)
    below = (
        lax.broadcasted_iota(jnp.int32, (tokens, tokens), 0)
        > lax.broadcasted_iota(jnp.int32, (tokens, tokens), 1)
    ).astype(f32).astype(jnp.bfloat16)
    earlier = lane.astype(f32) * cap
    places, place_rows, gates = [], [], []

    def column(ref, k):
        line = ref[k : k + 1, :].astype(f32)
        return jnp.transpose(jnp.broadcast_to(line, (128, tokens)))[:, :1]

    entries = lax.broadcasted_iota(jnp.int32, (tokens, table.shape[1]), 1)
    for k in range(ids.shape[0]):
        member = (column(ids, k) == lane.astype(f32)).astype(f32)
        rank = mm(below, member.astype(jnp.bfloat16)) + earlier
        place = jnp.sum(member * rank, axis=1, keepdims=True)
        earlier = earlier + jnp.sum(member, axis=0, keepdims=True)
        places.append(place)
        place_rows.append(jnp.transpose(jnp.broadcast_to(place, (tokens, 128)))[:1, :])
        chosen = column(gate_index, k) == entries.astype(f32)
        gates.append(jnp.sum(jnp.where(chosen, table[...], 0.0), axis=1, keepdims=True))

    def find_rows(e, _):
        slot = (lax.broadcasted_iota(jnp.int32, (cap, tokens), 0) + e * cap).astype(f32)
        hit = jnp.zeros((cap, tokens), f32)
        for row in place_rows:
            hit = hit + (slot == row).astype(f32)
        hits[pl.ds(pl.multiple_of(e * cap, cap), cap), :] = hit.astype(jnp.bfloat16)
        return 0

    lax.fori_loop(0, n, find_rows, 0)
    slot = lax.broadcasted_iota(jnp.int32, (tokens, n * cap), 1).astype(f32)
    for k, place in enumerate(places):
        picks[k] = (slot == place).astype(f32).astype(jnp.bfloat16)
        gate_of[k] = gates[k]

    for a in range(heads):
        here = slice(a * tokens, (a + 1) * tokens)
        queries[here, :] = q_latent[:, a * lat_width : (a + 1) * lat_width]
        rotary[here, :] = q_rotary[:, a * rope_width : (a + 1) * rope_width]

    def scores_of(lat, rope):
        return (mm(queries[...], lat) + mm(rotary[...], rope)) * score_scale

    lat = latent[...]
    scores = scores_of(lat, k_rotary[...])
    row = lax.broadcasted_iota(jnp.int32, (heads * tokens, tokens), 0)
    allowed = lax.broadcasted_iota(jnp.int32, scores.shape, 1) <= lax.rem(row, tokens)
    scores = jnp.where(allowed, scores, -1e30)
    peak = jnp.max(scores, axis=1, keepdims=True)
    weights = jnp.where(allowed, jnp.exp(scores - peak), 0.0)
    top[...] = peak
    norm[...] = jnp.sum(weights, axis=1, keepdims=True)
    acc[...] = mm_t(weights.astype(jnp.bfloat16), lat)

    second, third = 2, 4

    def block_of(s):
        share_keys(s, core, k2_s, k2_r, core).wait_recv()
        share_keys(s, diagonal, k4_s, k4_r, core).wait_recv()
        lat = keys[s, :, :lat_part, :].reshape(lat_width, tokens)
        return lat, keys[s, :, lat_part:, :].reshape(rope_width, tokens)

    def absorb(lat, rope):
        scores = scores_of(lat, rope)
        before = top[...]
        peak = jnp.maximum(before, jnp.max(scores, axis=1, keepdims=True))
        weights = jnp.exp(scores - peak)
        rescale = jnp.exp(before - peak)
        top[...] = peak
        norm[...] = norm[...] * rescale + jnp.sum(weights, axis=1, keepdims=True)
        acc[...] = acc[...] * rescale + mm_t(weights.astype(jnp.bfloat16), lat)

    def key_step(t, _):
        @pl.when(t <= c)
        def _():
            s, column = source_at(t)
            relay(s).wait_recv()

            @pl.when(column)
            def _():
                relay(s).start()
                relay_across(s).start()
                share_keys(s, h, k3_s, k3_r, across).start()

            share_keys(s, h, k2_s, k2_r, core).start()

        @pl.when((t > second) & (t <= c + second))
        def _():
            s, _ = source_at(t - second)
            share_keys(s, across, k3_s, k3_r, across).wait_recv()
            share_keys(s, across, k4_s, k4_r, core).start()

        w = t - third - y

        @pl.when((w == 0) & (y == 1))
        def _():
            absorb(*block_of(c - 1))

        @pl.when((w > 0) & (lax.rem(w, 2) == 0))
        def _():
            first, _ = source_at(t - third - 1)
            then, _ = source_at(t - third)
            blocks = zip(block_of(first), block_of(then))
            absorb(*[jnp.concatenate(pair, axis=1) for pair in blocks])

        return 0

    lax.fori_loop(1, c + 1 + third, key_step, 0)
    head_latent = (acc[...] / norm[...]).astype(jnp.bfloat16)
    loads[0].wait()
    loads[1].wait()
    head_value = jnp.concatenate(
        [
            mm(head_latent[a * tokens : (a + 1) * tokens, :], wv[a]).astype(jnp.bfloat16)
            for a in range(heads)
        ],
        axis=1,
    )

    def to_core(k):
        return remote(psend.at[k], ra.at[k], ra_s.at[k], ra_r.at[k], c, core)

    def to_across():
        return remote(rb_send, rb_recv, rb_s.at[0], rb_r.at[0], c, across)

    def dispatch(to):
        return remote(outgoing.at[to], arrived.at[h, c], d_s.at[to], d_r.at[c], to, h)

    def arrival(s):
        return remote(outgoing.at[s], arrived.at[h, s], d_s.at[s], d_r.at[s], s, h)

    def share_rows(j, g, send, recv, hd):
        part = arrived.at[g, pl.ds(j * per, per)]
        return remote(part, part, send.at[j], recv.at[j], c, hd)

    def take_chunk(j):
        def landed(k, _):
            i = j * per + k

            @pl.when(i != c)
            def _():
                arrival(i).wait_recv()

            return 0

        lax.fori_loop(0, per, landed, 0)
        share_rows(j, h, f2_s, f2_r, across).start()
        share_rows(j, h, f1_s, f1_r, core).start()

    def pass_chunk(j):
        share_rows(j, across, f2_s, f2_r, across).wait_recv()
        share_rows(j, across, f3_s, f3_r, core).start()

    mine = c // per
    mate = mine + 1 - 2 * lax.rem(mine, 2)

    def turn(p):
        if chunks < 8:
            return p
        third_pair = jnp.where(p == 2, mine, jnp.where(p == 3, mate, p - 2))
        last_pair = jnp.where(p == 2, mine, jnp.where(p == chunks - 1, mate, p - 1))
        third_pair = jnp.where((p < 2) | (p >= 6), p, third_pair)
        last_pair = jnp.where(p < 2, p, last_pair)
        order = jnp.where(mine >= 6, last_pair, third_pair)
        return jnp.where(mine >= 4, order, p)

    late = c // per >= chunks - 2
    lead = 2 * late.astype(jnp.int32)

    psend[1] = mm(head_value, wo[:, cols(diagonal)]).astype(jnp.bfloat16)
    to_core(1).start()
    across_part = mm(head_value, wo[:, cols(across)])
    to_core(1).wait_recv()
    rb_send[...] = (across_part + ra[1].astype(f32)).astype(jnp.bfloat16)
    to_across().start()
    psend[0] = mm(head_value, wo[:, cols(core)]).astype(jnp.bfloat16)
    to_core(0).start()
    own_part = mm(head_value, wo[:, cols(h)])
    loads[2].wait()
    to_core(0).wait_recv()
    base = hidden[:, cols(h)].astype(f32) + (own_part + ra[0].astype(f32))

    @pl.when(late)
    def _():
        take_chunk(0)
        take_chunk(1)

    to_across().wait_recv()
    attended = base + rb_recv[...].astype(f32)
    att[...] = attended
    scaled = (attended * gain[:, cols(h)]).astype(jnp.bfloat16)

    outgoing[...] = mm(hits[...], scaled).astype(jnp.bfloat16).reshape(n, cap, share)

    def send_rows(k, _):
        @pl.when(k != c)
        def _():
            dispatch(k).start()

        return 0

    held = c // per >= chunks - 2

    @pl.when(held)
    def _():
        lax.fori_loop(n // 2, n, send_rows, 0)

    upward = (c >= n // 4) & (c < n // 2)

    @pl.when(upward)
    def _():
        lax.fori_loop(0, n // 2, lambda k, _: send_rows(n // 2 + k, _), 0)

    lax.fori_loop(0, n // 2, send_rows, 0)

    @pl.when(jnp.logical_not(held | upward))
    def _():
        lax.fori_loop(n // 2, n, send_rows, 0)

    arrived[h, c] = outgoing[c]

    def y_core(j):
        return remote(ysend.at[j], yrecv.at[j], y_s.at[j], y_r.at[j], c, core)

    def y_across(j):
        return remote(xsend.at[j], xrecv.at[j], x_s.at[j], x_r.at[j], c, across)

    def give_back(s):
        return remote(back.at[s], returned.at[c], b_s.at[s], b_r.at[c], s, h)

    def come_home(e):
        return remote(back.at[e], returned.at[e], b_s.at[e], b_r.at[e], e, h)

    inverse_gain = 1.0 / gain[...]
    inverse_gain = inverse_gain * inverse_gain

    def step(t, _):
        @pl.when((t + 3 >= lead) & (t + 3 < chunks))
        def _():
            take_chunk(turn(t + 3))

        @pl.when((t + 1 >= 0) & (t + 1 < chunks))
        def _():
            pass_chunk(turn(t + 1))

        @pl.when((t >= 0) & (t < chunks))
        def _():
            j = turn(t)
            share_rows(j, core, f1_s, f1_r, core).wait_recv()
            share_rows(j, diagonal, f3_s, f3_r, core).wait_recv()
            gate_part = jnp.zeros((per * cap, wg.shape[0]), f32)
            up_part = jnp.zeros((per * cap, wg.shape[0]), f32)
            squares = jnp.zeros((per * cap, share), f32)
            for g in range(hd_count):
                here = slice(g * share, (g + 1) * share)
                rows = arrived[g, pl.ds(j * per, per)].reshape(per * cap, share)
                wide = rows.astype(f32)
                squares = squares + wide * wide * inverse_gain[:, here]
                gate_part = gate_part + mm_t(rows, wg[:, g * share : (g + 1) * share])
                up_part = up_part + mm_t(rows, wu[:, g * share : (g + 1) * share])
            mean = jnp.sum(squares, axis=1, keepdims=True) / model_width
            inverse = lax.rsqrt(mean + 1e-06)
            gate_part = gate_part * inverse
            up_part = up_part * inverse
            units = (gate_part / (1.0 + jnp.exp(-gate_part)) * up_part).astype(jnp.bfloat16)
            ysend[j, 0] = mm(units, wd[:, cols(core)]).astype(jnp.bfloat16)
            ysend[j, 1] = mm(units, wd[:, cols(diagonal)]).astype(jnp.bfloat16)
            y_core(j).start()
            yown[j, 0] = mm(units, wd[:, cols(h)])
            yown[j, 1] = mm(units, wd[:, cols(across)])

        @pl.when((t >= 1) & (t < chunks + 1))
        def _():
            j = turn(t - 1)
            y_core(j).wait_recv()
            xsend[j] = (yown[j, 1] + yrecv[j, 1].astype(f32)).astype(jnp.bfloat16)
            y_across(j).start()

        @pl.when(t >= 3)
        def _():
            j = turn(t - 3)
            y_across(j).wait_recv()
            whole = yown[j, 0] + yrecv[j, 0].astype(f32) + xrecv[j].astype(f32)
            back[pl.ds(j * per, per)] = whole.astype(jnp.bfloat16).reshape(per, cap, share)

            def go(k, _):
                i = j * per + k

                @pl.when(i != c)
                def _():
                    give_back(i).start()

                return 0

            lax.fori_loop(0, per, go, 0)

        return 0

    for load in loads[3:]:
        load.wait()
    lax.fori_loop(-3, chunks + 3, step, 0)
    returned[c] = back[c]

    def home(i, _):
        come_home(lax.rem(c + i, n)).wait_recv()
        return 0

    lax.fori_loop(1, n, home, 0)
    rows = returned[...].reshape(n * cap, share)
    mixed = att[...]
    for k in range(len(places)):
        mixed = mixed + gate_of[k] * mm(picks[k], rows)
    out[...] = mixed.astype(out.dtype)

    def sent_keys(k, _):
        to_column(k).wait_send()
        return 0

    def sent_relays(k, _):
        s = 2 * k + y
        relay(s).wait_send()
        relay_across(s).wait_send()
        share_keys(s, h, k3_s, k3_r, across).wait_send()
        return 0

    def sent_shares(i, _):
        share_keys(i, h, k2_s, k2_r, core).wait_send()
        share_keys(i, across, k4_s, k4_r, core).wait_send()
        return 0

    @pl.when(y == 0)
    def _():
        to_partner().wait_send()
        second_to_partner().wait_send()

    lax.fori_loop(z + 1, n // 2, sent_keys, 0)
    lax.fori_loop(0, z, sent_relays, 0)
    lax.fori_loop(0, c, sent_shares, 0)
    to_core(0).wait_send()
    to_core(1).wait_send()
    to_across().wait_send()

    def sent(i, _):
        to = lax.rem(c + i, n)
        give_back(to).wait_send()
        dispatch(to).wait_send()
        return 0

    lax.fori_loop(1, n, sent, 0)

    def sent_chunk(j, _):
        share_rows(j, h, f1_s, f1_r, core).wait_send()
        share_rows(j, h, f2_s, f2_r, across).wait_send()
        share_rows(j, across, f3_s, f3_r, core).wait_send()
        y_core(j).wait_send()
        y_across(j).wait_send()
        return 0

    lax.fori_loop(0, chunks, sent_chunk, 0)


def on_device(
    hidden_in,
    q_latent,
    q_rotary,
    latent,
    k_rotary,
    w_value,
    w_output,
    ffn_gain,
    w_gate,
    w_up,
    w_down,
    expert_ids,
    gate_index,
    gate_table,
):
    n, hd_count = lax.axis_size("ctx"), lax.axis_size("hd")
    tokens, width = hidden_in.shape
    share = width // hd_count
    needed = 3 * tokens * expert_ids.shape[1] // (2 * n * w_gate.shape[0])
    cap = (needed + 15) // 16 * 16
    chunks = math.gcd(n, 8)
    rows = n // chunks * cap
    bf = jnp.bfloat16
    f32 = jnp.float32
    vm = pltpu.VMEM
    lat_width, rope_width = latent.shape[0], k_rotary.shape[0]
    stacked = w_value.shape[0] * tokens
    quarter = (lat_width + rope_width) // hd_count
    return pl.pallas_call(
        functools.partial(layer_kernel, n, chunks, width),
        out_shape=jax.ShapeDtypeStruct((tokens, share), bf),
        in_specs=[pl.BlockSpec(memory_space=pltpu.VMEM)] * 8
        + [pl.BlockSpec(memory_space=pl.ANY)] * 6,
        out_specs=pl.BlockSpec(memory_space=pltpu.VMEM),
        scratch_shapes=[
            vm(hidden_in.shape, bf),
            vm(w_value.shape, bf),
            vm(w_output.shape, bf),
            vm(w_gate.shape[:0:-1], bf),
            vm(w_up.shape[:0:-1], bf),
            vm(w_down.shape[1:], bf),
            vm((hd_count, quarter, tokens), bf),
            vm((n, hd_count, quarter, tokens), bf),
            vm((stacked, lat_width), bf),
            vm((stacked, rope_width), bf),
            vm((stacked, 1), f32),
            vm((stacked, 1), f32),
            vm((stacked, lat_width), f32),
            vm((n * cap, tokens), bf),
            vm((expert_ids.shape[1], tokens, n * cap), bf),
            vm((expert_ids.shape[1], tokens, 1), f32),
            vm((2, tokens, share), bf),
            vm((2, tokens, share), bf),
            vm((tokens, share), bf),
            vm((tokens, share), bf),
            vm((tokens, share), f32),
            vm((n, cap, share), bf),
            vm((hd_count, n, cap, share), bf),
            vm((chunks, 2, rows, share), f32),
            vm((chunks, 2, rows, share), bf),
            vm((chunks, 2, rows, share), bf),
            vm((chunks, rows, share), bf),
            vm((chunks, rows, share), bf),
            vm((n, cap, share), bf),
            vm((n, cap, share), bf),
        ]
        + [DMA((6,)), DMA((1,))]
        + [DMA((n,))] * 10
        + [DMA((2,))] * 2
        + [DMA((1,))] * 2
        + [DMA((n,))] * 2
        + [DMA((chunks,))] * 10
        + [DMA((n,))] * 2,
        compiler_params=pltpu.CompilerParams(
            collective_id=0, has_side_effects=True, vmem_limit_bytes=60 * 1024 * 1024
        ),
    )(
        q_latent,
        q_rotary,
        latent,
        k_rotary,
        ffn_gain[None, :],
        expert_ids.T,
        gate_index.T,
        gate_table[None, :],
        hidden_in,
        w_value,
        w_output,
        jnp.swapaxes(w_gate, 1, 2),
        jnp.swapaxes(w_up, 1, 2),
        w_down,
    )


def solution(mesh):
    in_specs = (
        P("ctx", None),
        P("ctx", "hd"),
        P("ctx", "hd"),
        P(None, "ctx"),
        P(None, "ctx"),
        P("hd", None, None),
        P("hd", None),
        P(),
        P("ctx", None, "hd"),
        P("ctx", None, "hd"),
        P("ctx", "hd", None),
        P("ctx", None),
        P("ctx", None),
        P(),
    )
    out_specs = P("ctx", "hd")
    return jax.shard_map(
        on_device, mesh=mesh, in_specs=in_specs, out_specs=out_specs, check_vma=False
    )
```

```python
import functools
import math

import jax
import jax.numpy as jnp
from jax import lax
from jax.experimental import pallas as pl
from jax.experimental.pallas import tpu as pltpu
from jax.sharding import PartitionSpec as P

ROPE = 64
NOPE = 128

MESH = pl.DeviceIdType.MESH
DMA = pltpu.SemaphoreType.DMA


def neighbours():
    h = lax.axis_index("hd")
    return h + 1 - 2 * lax.rem(h, 2), h + 2 - 4 * (h // 2)


def remote(src, dst, send, recv, ctx, hd):
    return pltpu.make_async_remote_copy(
        src_ref=src,
        dst_ref=dst,
        send_sem=send,
        recv_sem=recv,
        device_id={"ctx": ctx, "hd": hd},
        device_id_type=MESH,
    )


def greet(n, hd_count):
    c, h = lax.axis_index("ctx"), lax.axis_index("hd")
    barrier = pltpu.get_barrier_semaphore()

    def over_ctx(i, _):
        peer = {"ctx": lax.rem(c + i, n), "hd": h}
        pl.semaphore_signal(barrier, inc=1, device_id=peer, device_id_type=MESH)
        return 0

    lax.fori_loop(1, n, over_ctx, 0)
    for i in range(1, hd_count):
        peer = {"ctx": c, "hd": lax.rem(h + i, hd_count)}
        pl.semaphore_signal(barrier, inc=1, device_id=peer, device_id_type=MESH)
    peer = {"ctx": c + 1 - 2 * lax.rem(c, 2), "hd": neighbours()[1]}
    pl.semaphore_signal(barrier, inc=1, device_id=peer, device_id_type=MESH)
    pl.semaphore_wait(barrier, n + hd_count - 1)


def mm(a, b):
    return jnp.dot(a, b, preferred_element_type=jnp.float32)


def mm_t(a, b):
    return lax.dot_general(a, b, (((1,), (1,)), ((), ())), preferred_element_type=jnp.float32)


def layer_kernel(
    n, chunks, model_width,
    q_rotary, gain, ids, gate_index, table,
    q_latent, latent, k_rotary, hidden_hbm, wv_hbm, wo_hbm, wg_hbm, wu_hbm, wd_hbm,
    out,
    hidden, wv, wo, wg, wu, wd,
    src, keys, queries, rotary, top, norm, acc, hits, picks, gate_of,
    psend, ra, rb_send, rb_recv, att, outgoing, arrived,
    yown, ysend, yrecv, xsend, xrecv, back, returned,
    q_s, w_s, kw_s, k1_s, k1_r, kr_s, kx_s, k2_s, k2_r, k3_s, k3_r, k4_s, k4_r,
    ra_s, ra_r, rb_s, rb_r, d_s, d_r,
    f1_s, f1_r, f2_s, f2_r, f3_s, f3_r, y_s, y_r, x_s, x_r, b_s, b_r,
):
    c, h = lax.axis_index("ctx"), lax.axis_index("hd")
    core, across = neighbours()
    diagonal = core + across - h
    share = out.shape[1]
    cap = outgoing.shape[1]
    per = n // chunks
    hd_count = model_width // share
    f32 = jnp.float32

    def cols(g):
        return pl.ds(pl.multiple_of(g * share, share), share)

    heads = wv.shape[0]
    lat_width, tokens = latent.shape
    rope_width = k_rotary.shape[0]
    lat_part, rope_part = lat_width // hd_count, rope_width // hd_count
    score_scale = 1.0 / math.sqrt(NOPE + ROPE)

    pieces = []
    for g in range(hd_count):
        pieces.append((latent.at[g * lat_part : (g + 1) * lat_part], src.at[g, :lat_part]))
        pieces.append((k_rotary.at[g * rope_part : (g + 1) * rope_part], src.at[g, lat_part:]))
    for a in range(heads):
        here = pl.ds(a * tokens, tokens)
        lat_cols = pl.ds(a * lat_width, lat_width)
        pieces.append((q_latent.at[:, lat_cols], queries.at[here]))
    inputs = [pltpu.make_async_copy(a, b, q_s.at[k]) for k, (a, b) in enumerate(pieces)]
    for piece in inputs:
        piece.start()
    loads = [
        pltpu.make_async_copy(a, b, w_s.at[k])
        for k, (a, b) in enumerate(
            [(wv_hbm, wv), (wo_hbm, wo), (hidden_hbm, hidden), (wg_hbm.at[0], wg),
             (wu_hbm.at[0], wu), (wd_hbm.at[0], wd)]
        )
    ]
    for load in loads:
        load.start()
    greet(n, hd_count)
    for piece in inputs[: 2 * hd_count]:
        piece.wait()

    z, y = c // 2, lax.rem(c, 2)
    partner = c + 1 - 2 * y

    def to_column(k):
        return remote(src.at[h], keys.at[c, h], k1_s.at[k], k1_r.at[c], 2 * k + y, h)

    def to_partner():
        return remote(src.at[h], keys.at[c, h], k1_s.at[z], k1_r.at[c], partner, h)

    def second_to_partner():
        return remote(src.at[across], keys.at[c, across], kw_s.at[0], k3_r.at[c], partner, h)

    def relay(s):
        piece = keys.at[s, h]
        return remote(piece, piece, kr_s.at[s], k1_r.at[s], partner, h)

    def relay_across(s):
        piece = keys.at[s, h]
        return remote(piece, piece, kx_s.at[s], k3_r.at[s], partner, across)

    def share_keys(s, quarter, send, recv, hd):
        piece = keys.at[s, quarter]
        return remote(piece, piece, send.at[s], recv.at[s], c, hd)

    def source_at(t):
        w = t - y
        column = (w >= 1) & (w <= z)
        depth = w - z * (w > z).astype(jnp.int32)
        other = 1 - column.astype(jnp.int32)
        return 2 * (z - depth) + y + other * (1 - 2 * y), column

    def start_keys(k, _):
        to_column(k).start()
        return 0

    @pl.when(y == 0)
    def _():
        to_partner().start()
        second_to_partner().start()

    lax.fori_loop(z + 1, n // 2, start_keys, 0)
    width = (n + 127) // 128 * 128
    lane = lax.broadcasted_iota(jnp.int32, (tokens, width), 1)
    below = (
        lax.broadcasted_iota(jnp.int32, (tokens, tokens), 0)
        > lax.broadcasted_iota(jnp.int32, (tokens, tokens), 1)
    ).astype(f32).astype(jnp.bfloat16)
    earlier = lane.astype(f32) * cap
    places, place_rows, gates = [], [], []

    def column(ref, k):
        line = ref[k : k + 1, :].astype(f32)
        return jnp.transpose(jnp.broadcast_to(line, (128, tokens)))[:, :1]

    entries = lax.broadcasted_iota(jnp.int32, (tokens, table.shape[1]), 1)
    for k in range(ids.shape[0]):
        member = (column(ids, k) == lane.astype(f32)).astype(f32)
        rank = mm(below, member.astype(jnp.bfloat16)) + earlier
        place = jnp.sum(member * rank, axis=1, keepdims=True)
        earlier = earlier + jnp.sum(member, axis=0, keepdims=True)
        places.append(place)
        place_rows.append(jnp.transpose(jnp.broadcast_to(place, (tokens, 128)))[:1, :])
        chosen = column(gate_index, k) == entries.astype(f32)
        gates.append(jnp.sum(jnp.where(chosen, table[...], 0.0), axis=1, keepdims=True))

    def find_rows(e, _):
        slot = (lax.broadcasted_iota(jnp.int32, (cap, tokens), 0) + e * cap).astype(f32)
        hit = jnp.zeros((cap, tokens), f32)
        for row in place_rows:
            hit = hit + (slot == row).astype(f32)
        hits[pl.ds(pl.multiple_of(e * cap, cap), cap), :] = hit.astype(jnp.bfloat16)
        return 0

    lax.fori_loop(0, n, find_rows, 0)
    slot = lax.broadcasted_iota(jnp.int32, (tokens, n * cap), 1).astype(f32)
    for k, place in enumerate(places):
        picks[k] = (slot == place).astype(f32).astype(jnp.bfloat16)
        gate_of[k] = gates[k]

    for a in range(heads):
        here = slice(a * tokens, (a + 1) * tokens)
        rotary[here, :] = q_rotary[:, a * rope_width : (a + 1) * rope_width]
    for piece in inputs[2 * hd_count :]:
        piece.wait()

    def scores_of(lat, rope):
        return (mm(queries[...], lat) + mm(rotary[...], rope)) * score_scale

    lat = src[:, :lat_part, :].reshape(lat_width, tokens)
    scores = scores_of(lat, src[:, lat_part:, :].reshape(rope_width, tokens))
    row = lax.broadcasted_iota(jnp.int32, (heads * tokens, tokens), 0)
    allowed = lax.broadcasted_iota(jnp.int32, scores.shape, 1) <= lax.rem(row, tokens)
    scores = jnp.where(allowed, scores, -1e30)
    peak = jnp.max(scores, axis=1, keepdims=True)
    weights = jnp.where(allowed, jnp.exp(scores - peak), 0.0)
    top[...] = peak
    norm[...] = jnp.sum(weights, axis=1, keepdims=True)
    acc[...] = mm_t(weights.astype(jnp.bfloat16), lat)

    second, third = 2, 4

    def block_of(s):
        share_keys(s, core, k2_s, k2_r, core).wait_recv()
        share_keys(s, diagonal, k4_s, k4_r, core).wait_recv()
        lat = keys[s, :, :lat_part, :].reshape(lat_width, tokens)
        return lat, keys[s, :, lat_part:, :].reshape(rope_width, tokens)

    def absorb(lat, rope):
        scores = scores_of(lat, rope)
        before = top[...]
        peak = jnp.maximum(before, jnp.max(scores, axis=1, keepdims=True))
        weights = jnp.exp(scores - peak)
        rescale = jnp.exp(before - peak)
        top[...] = peak
        norm[...] = norm[...] * rescale + jnp.sum(weights, axis=1, keepdims=True)
        acc[...] = acc[...] * rescale + mm_t(weights.astype(jnp.bfloat16), lat)

    def key_step(t, _):
        @pl.when(t <= c)
        def _():
            s, column = source_at(t)
            relay(s).wait_recv()

            @pl.when(column)
            def _():
                relay(s).start()
                relay_across(s).start()
                share_keys(s, h, k3_s, k3_r, across).start()

            share_keys(s, h, k2_s, k2_r, core).start()

        @pl.when((t > second) & (t <= c + second))
        def _():
            s, _ = source_at(t - second)
            share_keys(s, across, k3_s, k3_r, across).wait_recv()
            share_keys(s, across, k4_s, k4_r, core).start()

        w = t - third - y

        @pl.when((w == 0) & (y == 1))
        def _():
            absorb(*block_of(c - 1))

        @pl.when((w > 0) & (lax.rem(w, 2) == 0))
        def _():
            first, _ = source_at(t - third - 1)
            then, _ = source_at(t - third)
            blocks = zip(block_of(first), block_of(then))
            absorb(*[jnp.concatenate(pair, axis=1) for pair in blocks])

        return 0

    lax.fori_loop(1, c + 1 + third, key_step, 0)
    head_latent = (acc[...] / norm[...]).astype(jnp.bfloat16)
    loads[0].wait()
    loads[1].wait()
    head_value = jnp.concatenate(
        [
            mm(head_latent[a * tokens : (a + 1) * tokens, :], wv[a]).astype(jnp.bfloat16)
            for a in range(heads)
        ],
        axis=1,
    )

    def to_core(k):
        return remote(psend.at[k], ra.at[k], ra_s.at[k], ra_r.at[k], c, core)

    def to_across():
        return remote(rb_send, rb_recv, rb_s.at[0], rb_r.at[0], c, across)

    def dispatch(to):
        return remote(outgoing.at[to], arrived.at[h, c], d_s.at[to], d_r.at[c], to, h)

    def arrival(s):
        return remote(outgoing.at[s], arrived.at[h, s], d_s.at[s], d_r.at[s], s, h)

    def share_rows(j, g, send, recv, hd):
        part = arrived.at[g, pl.ds(j * per, per)]
        return remote(part, part, send.at[j], recv.at[j], c, hd)

    def take_chunk(j):
        def landed(k, _):
            i = j * per + k

            @pl.when(i != c)
            def _():
                arrival(i).wait_recv()

            return 0

        lax.fori_loop(0, per, landed, 0)
        share_rows(j, h, f2_s, f2_r, across).start()
        share_rows(j, h, f1_s, f1_r, core).start()

    def pass_chunk(j):
        share_rows(j, across, f2_s, f2_r, across).wait_recv()
        share_rows(j, across, f3_s, f3_r, core).start()

    mine = c // per
    mate = mine + 1 - 2 * lax.rem(mine, 2)

    def turn(p):
        if chunks < 8:
            return p
        third_pair = jnp.where(p == 2, mine, jnp.where(p == 3, mate, p - 2))
        last_pair = jnp.where(p == 3, mate, jnp.where(p == chunks - 1, mine, p - (p > 3).astype(jnp.int32)))
        third_pair = jnp.where(p >= 6, p - 4, jnp.where(p >= 4, p + 2, third_pair))
        third_pair = jnp.where(p < 2, p, third_pair)
        last_pair = jnp.where(p < 2, p, last_pair)
        order = jnp.where(mine >= 6, last_pair, third_pair)
        return jnp.where(mine >= 4, order, p)

    late = c // per >= chunks - 2
    lead = 2 * late.astype(jnp.int32)

    psend[1] = mm(head_value, wo[:, cols(diagonal)]).astype(jnp.bfloat16)
    to_core(1).start()
    across_part = mm(head_value, wo[:, cols(across)])
    to_core(1).wait_recv()
    rb_send[...] = (across_part + ra[1].astype(f32)).astype(jnp.bfloat16)
    to_across().start()
    psend[0] = mm(head_value, wo[:, cols(core)]).astype(jnp.bfloat16)
    to_core(0).start()
    own_part = mm(head_value, wo[:, cols(h)])
    loads[2].wait()
    to_core(0).wait_recv()
    base = hidden[:, cols(h)].astype(f32) + (own_part + ra[0].astype(f32))

    @pl.when(late)
    def _():
        take_chunk(0)
        take_chunk(1)

    to_across().wait_recv()
    attended = base + rb_recv[...].astype(f32)
    att[...] = attended
    scaled = (attended * gain[:, cols(h)]).astype(jnp.bfloat16)

    outgoing[...] = mm(hits[...], scaled).astype(jnp.bfloat16).reshape(n, cap, share)

    def send_rows(k, _):
        @pl.when(k != c)
        def _():
            dispatch(k).start()

        return 0

    held = c // per >= chunks - 2

    @pl.when(held)
    def _():
        lax.fori_loop(n // 2, n, send_rows, 0)

    upward = (c >= n // 4) & (c < n // 2)

    @pl.when(upward)
    def _():
        lax.fori_loop(0, n // 2, lambda k, _: send_rows(n // 2 + k, _), 0)

    lax.fori_loop(0, n // 2, send_rows, 0)

    @pl.when(jnp.logical_not(held | upward))
    def _():
        lax.fori_loop(n // 2, n, send_rows, 0)

    arrived[h, c] = outgoing[c]

    def y_core(j):
        return remote(ysend.at[j], yrecv.at[j], y_s.at[j], y_r.at[j], c, core)

    def y_across(j):
        return remote(xsend.at[j], xrecv.at[j], x_s.at[j], x_r.at[j], c, across)

    def give_back(s):
        return remote(back.at[s], returned.at[c], b_s.at[s], b_r.at[c], s, h)

    def come_home(e):
        return remote(back.at[e], returned.at[e], b_s.at[e], b_r.at[e], e, h)

    inverse_gain = 1.0 / gain[...]
    inverse_gain = inverse_gain * inverse_gain

    def step(t, _):
        @pl.when((t + 3 >= lead) & (t + 3 < chunks))
        def _():
            take_chunk(turn(t + 3))

        @pl.when((t + 1 >= 0) & (t + 1 < chunks))
        def _():
            pass_chunk(turn(t + 1))

        @pl.when((t >= 0) & (t < chunks))
        def _():
            j = turn(t)
            share_rows(j, core, f1_s, f1_r, core).wait_recv()
            share_rows(j, diagonal, f3_s, f3_r, core).wait_recv()
            shares = [
                arrived[g, pl.ds(j * per, per)].reshape(per * cap, share) for g in range(hd_count)
            ]
            squares = jnp.zeros((per * cap, share), f32)
            for g, rows in enumerate(shares):
                wide = rows.astype(f32)
                squares = squares + wide * wide * inverse_gain[:, g * share : (g + 1) * share]
            rows = jnp.concatenate(shares, axis=1)
            gate_part = mm_t(rows, wg[...])
            up_part = mm_t(rows, wu[...])
            mean = jnp.sum(squares, axis=1, keepdims=True) / model_width
            inverse = lax.rsqrt(mean + 1e-06)
            gate_part = gate_part * inverse
            up_part = up_part * inverse
            units = (gate_part / (1.0 + jnp.exp(-gate_part)) * up_part).astype(jnp.bfloat16)
            ysend[j, 0] = mm(units, wd[:, cols(core)]).astype(jnp.bfloat16)
            ysend[j, 1] = mm(units, wd[:, cols(diagonal)]).astype(jnp.bfloat16)
            y_core(j).start()
            yown[j, 0] = mm(units, wd[:, cols(h)])
            yown[j, 1] = mm(units, wd[:, cols(across)])

        @pl.when((t >= 1) & (t < chunks + 1))
        def _():
            j = turn(t - 1)
            y_core(j).wait_recv()
            xsend[j] = (yown[j, 1] + yrecv[j, 1].astype(f32)).astype(jnp.bfloat16)
            y_across(j).start()

        @pl.when(t >= 3)
        def _():
            j = turn(t - 3)
            y_across(j).wait_recv()
            whole = yown[j, 0] + yrecv[j, 0].astype(f32) + xrecv[j].astype(f32)
            back[pl.ds(j * per, per)] = whole.astype(jnp.bfloat16).reshape(per, cap, share)

            def go(k, _):
                i = j * per + k

                @pl.when(i != c)
                def _():
                    give_back(i).start()

                return 0

            lax.fori_loop(0, per, go, 0)

        return 0

    for load in loads[3:]:
        load.wait()
    lax.fori_loop(-3, chunks + 3, step, 0)
    returned[c] = back[c]

    def home(i, _):
        come_home(lax.rem(c + i, n)).wait_recv()
        return 0

    lax.fori_loop(1, n, home, 0)
    rows = returned[...].reshape(n * cap, share)
    mixed = att[...]
    for k in range(len(places)):
        mixed = mixed + gate_of[k] * mm(picks[k], rows)
    out[...] = mixed.astype(out.dtype)

    def sent_keys(k, _):
        to_column(k).wait_send()
        return 0

    def sent_relays(k, _):
        s = 2 * k + y
        relay(s).wait_send()
        relay_across(s).wait_send()
        share_keys(s, h, k3_s, k3_r, across).wait_send()
        return 0

    def sent_shares(i, _):
        share_keys(i, h, k2_s, k2_r, core).wait_send()
        share_keys(i, across, k4_s, k4_r, core).wait_send()
        return 0

    @pl.when(y == 0)
    def _():
        to_partner().wait_send()
        second_to_partner().wait_send()

    lax.fori_loop(z + 1, n // 2, sent_keys, 0)
    lax.fori_loop(0, z, sent_relays, 0)
    lax.fori_loop(0, c, sent_shares, 0)
    to_core(0).wait_send()
    to_core(1).wait_send()
    to_across().wait_send()

    def sent(i, _):
        to = lax.rem(c + i, n)
        give_back(to).wait_send()
        dispatch(to).wait_send()
        return 0

    lax.fori_loop(1, n, sent, 0)

    def sent_chunk(j, _):
        share_rows(j, h, f1_s, f1_r, core).wait_send()
        share_rows(j, h, f2_s, f2_r, across).wait_send()
        share_rows(j, across, f3_s, f3_r, core).wait_send()
        y_core(j).wait_send()
        y_across(j).wait_send()
        return 0

    lax.fori_loop(0, chunks, sent_chunk, 0)


def on_device(
    hidden_in,
    q_latent,
    q_rotary,
    latent,
    k_rotary,
    w_value,
    w_output,
    ffn_gain,
    w_gate,
    w_up,
    w_down,
    expert_ids,
    gate_index,
    gate_table,
):
    n, hd_count = lax.axis_size("ctx"), lax.axis_size("hd")
    tokens, width = hidden_in.shape
    share = width // hd_count
    needed = 3 * tokens * expert_ids.shape[1] // (2 * n * w_gate.shape[0])
    cap = (needed + 15) // 16 * 16
    chunks = math.gcd(n, 8)
    rows = n // chunks * cap
    bf = jnp.bfloat16
    f32 = jnp.float32
    vm = pltpu.VMEM
    lat_width, rope_width = latent.shape[0], k_rotary.shape[0]
    stacked = w_value.shape[0] * tokens
    quarter = (lat_width + rope_width) // hd_count
    return pl.pallas_call(
        functools.partial(layer_kernel, n, chunks, width),
        out_shape=jax.ShapeDtypeStruct((tokens, share), bf),
        in_specs=[pl.BlockSpec(memory_space=pltpu.VMEM)] * 5
        + [pl.BlockSpec(memory_space=pl.ANY)] * 9,
        out_specs=pl.BlockSpec(memory_space=pltpu.VMEM),
        scratch_shapes=[
            vm(hidden_in.shape, bf),
            vm(w_value.shape, bf),
            vm(w_output.shape, bf),
            vm(w_gate.shape[:0:-1], bf),
            vm(w_up.shape[:0:-1], bf),
            vm(w_down.shape[1:], bf),
            vm((hd_count, quarter, tokens), bf),
            vm((n, hd_count, quarter, tokens), bf),
            vm((stacked, lat_width), bf),
            vm((stacked, rope_width), bf),
            vm((stacked, 1), f32),
            vm((stacked, 1), f32),
            vm((stacked, lat_width), f32),
            vm((n * cap, tokens), bf),
            vm((expert_ids.shape[1], tokens, n * cap), bf),
            vm((expert_ids.shape[1], tokens, 1), f32),
            vm((2, tokens, share), bf),
            vm((2, tokens, share), bf),
            vm((tokens, share), bf),
            vm((tokens, share), bf),
            vm((tokens, share), f32),
            vm((n, cap, share), bf),
            vm((hd_count, n, cap, share), bf),
            vm((chunks, 2, rows, share), f32),
            vm((chunks, 2, rows, share), bf),
            vm((chunks, 2, rows, share), bf),
            vm((chunks, rows, share), bf),
            vm((chunks, rows, share), bf),
            vm((n, cap, share), bf),
            vm((n, cap, share), bf),
        ]
        + [DMA((2 * hd_count + w_value.shape[0],)), DMA((6,)), DMA((1,))]
        + [DMA((n,))] * 10
        + [DMA((2,))] * 2
        + [DMA((1,))] * 2
        + [DMA((n,))] * 2
        + [DMA((chunks,))] * 10
        + [DMA((n,))] * 2,
        compiler_params=pltpu.CompilerParams(
            collective_id=0, has_side_effects=True, vmem_limit_bytes=60 * 1024 * 1024
        ),
    )(
        q_rotary,
        ffn_gain[None, :],
        expert_ids.T,
        gate_index.T,
        gate_table[None, :],
        q_latent,
        latent,
        k_rotary,
        hidden_in,
        w_value,
        w_output,
        jnp.swapaxes(w_gate, 1, 2),
        jnp.swapaxes(w_up, 1, 2),
        w_down,
    )


def solution(mesh):
    in_specs = (
        P("ctx", None),
        P("ctx", "hd"),
        P("ctx", "hd"),
        P(None, "ctx"),
        P(None, "ctx"),
        P("hd", None, None),
        P("hd", None),
        P(),
        P("ctx", None, "hd"),
        P("ctx", None, "hd"),
        P("ctx", "hd", None),
        P("ctx", None),
        P("ctx", None),
        P(),
    )
    out_specs = P("ctx", "hd")
    return jax.shard_map(
        on_device, mesh=mesh, in_specs=in_specs, out_specs=out_specs, check_vma=False
    )
```

```python
import functools
import math

import jax
import jax.numpy as jnp
from jax import lax
from jax.experimental import pallas as pl
from jax.experimental.pallas import tpu as pltpu
from jax.sharding import PartitionSpec as P

ROPE = 64
NOPE = 128

MESH = pl.DeviceIdType.MESH
DMA = pltpu.SemaphoreType.DMA


def neighbours():
    h = lax.axis_index("hd")
    return h + 1 - 2 * lax.rem(h, 2), h + 2 - 4 * (h // 2)


def remote(src, dst, send, recv, ctx, hd):
    return pltpu.make_async_remote_copy(
        src_ref=src,
        dst_ref=dst,
        send_sem=send,
        recv_sem=recv,
        device_id={"ctx": ctx, "hd": hd},
        device_id_type=MESH,
    )


def greet(n, hd_count):
    c, h = lax.axis_index("ctx"), lax.axis_index("hd")
    barrier = pltpu.get_barrier_semaphore()

    def over_ctx(i, _):
        peer = {"ctx": lax.rem(c + i, n), "hd": h}
        pl.semaphore_signal(barrier, inc=1, device_id=peer, device_id_type=MESH)
        return 0

    lax.fori_loop(1, n, over_ctx, 0)
    for i in range(1, hd_count):
        peer = {"ctx": c, "hd": lax.rem(h + i, hd_count)}
        pl.semaphore_signal(barrier, inc=1, device_id=peer, device_id_type=MESH)
    peer = {"ctx": c + 1 - 2 * lax.rem(c, 2), "hd": neighbours()[1]}
    pl.semaphore_signal(barrier, inc=1, device_id=peer, device_id_type=MESH)
    pl.semaphore_wait(barrier, n + hd_count - 1)


def mm(a, b):
    return jnp.dot(a, b, preferred_element_type=jnp.float32)


def mm_t(a, b):
    return lax.dot_general(a, b, (((1,), (1,)), ((), ())), preferred_element_type=jnp.float32)


def layer_kernel(
    n, chunks, model_width,
    q_rotary, gain, ids, gate_index, table,
    q_latent, latent, k_rotary, hidden_hbm, wv_hbm, wo_hbm, wg_hbm, wu_hbm, wd_hbm,
    out,
    hidden, wv, wo, wg, wu, wd,
    src, keys, queries, rotary, top, norm, acc, hits, picks, gate_of,
    psend, ra, rb_send, rb_recv, att, outgoing, arrived,
    yown, ysend, yrecv, xsend, xrecv, back, returned,
    q_s, w_s, kw_s, k1_s, k1_r, kr_s, kx_s, k2_s, k2_r, k3_s, k3_r, k4_s, k4_r,
    ra_s, ra_r, rb_s, rb_r, d_s, d_r,
    f1_s, f1_r, f2_s, f2_r, f3_s, f3_r, y_s, y_r, yd_s, yd_r, x_s, x_r, b_s, b_r,
):
    c, h = lax.axis_index("ctx"), lax.axis_index("hd")
    core, across = neighbours()
    diagonal = core + across - h
    share = out.shape[1]
    cap = outgoing.shape[1]
    per = n // chunks
    hd_count = model_width // share
    f32 = jnp.float32

    def cols(g):
        return pl.ds(pl.multiple_of(g * share, share), share)

    heads = wv.shape[0]
    lat_width, tokens = latent.shape
    rope_width = k_rotary.shape[0]
    lat_part, rope_part = lat_width // hd_count, rope_width // hd_count
    score_scale = 1.0 / math.sqrt(NOPE + ROPE)

    pieces = []
    for g in range(hd_count):
        pieces.append((latent.at[g * lat_part : (g + 1) * lat_part], src.at[g, :lat_part]))
        pieces.append((k_rotary.at[g * rope_part : (g + 1) * rope_part], src.at[g, lat_part:]))
    for a in range(heads):
        here = pl.ds(a * tokens, tokens)
        lat_cols = pl.ds(a * lat_width, lat_width)
        pieces.append((q_latent.at[:, lat_cols], queries.at[here]))
    inputs = [pltpu.make_async_copy(a, b, q_s.at[k]) for k, (a, b) in enumerate(pieces)]
    for piece in inputs:
        piece.start()
    loads = [
        pltpu.make_async_copy(a, b, w_s.at[k])
        for k, (a, b) in enumerate(
            [(wv_hbm, wv), (wo_hbm, wo), (hidden_hbm, hidden), (wg_hbm.at[0], wg),
             (wu_hbm.at[0], wu), (wd_hbm.at[0], wd)]
        )
    ]
    for load in loads:
        load.start()
    greet(n, hd_count)
    for piece in inputs[: 2 * hd_count]:
        piece.wait()

    z, y = c // 2, lax.rem(c, 2)
    partner = c + 1 - 2 * y

    def to_column(k):
        return remote(src.at[h], keys.at[c, h], k1_s.at[k], k1_r.at[c], 2 * k + y, h)

    def to_partner():
        return remote(src.at[h], keys.at[c, h], k1_s.at[z], k1_r.at[c], partner, h)

    def second_to_partner():
        return remote(src.at[across], keys.at[c, across], kw_s.at[0], k3_r.at[c], partner, h)

    def relay(s):
        piece = keys.at[s, h]
        return remote(piece, piece, kr_s.at[s], k1_r.at[s], partner, h)

    def relay_across(s):
        piece = keys.at[s, h]
        return remote(piece, piece, kx_s.at[s], k3_r.at[s], partner, across)

    def share_keys(s, quarter, send, recv, hd):
        piece = keys.at[s, quarter]
        return remote(piece, piece, send.at[s], recv.at[s], c, hd)

    def source_at(t):
        w = t - y
        column = (w >= 1) & (w <= z)
        depth = w - z * (w > z).astype(jnp.int32)
        other = 1 - column.astype(jnp.int32)
        return 2 * (z - depth) + y + other * (1 - 2 * y), column

    def start_keys(k, _):
        to_column(k).start()
        return 0

    @pl.when(y == 0)
    def _():
        to_partner().start()
        second_to_partner().start()

    lax.fori_loop(z + 1, n // 2, start_keys, 0)
    for a in range(heads):
        here = slice(a * tokens, (a + 1) * tokens)
        rotary[here, :] = q_rotary[:, a * rope_width : (a + 1) * rope_width]
    for piece in inputs[2 * hd_count :]:
        piece.wait()

    def scores_of(lat, rope):
        return (mm(queries[...], lat) + mm(rotary[...], rope)) * score_scale

    lat = src[:, :lat_part, :].reshape(lat_width, tokens)
    scores = scores_of(lat, src[:, lat_part:, :].reshape(rope_width, tokens))
    row = lax.broadcasted_iota(jnp.int32, (heads * tokens, tokens), 0)
    allowed = lax.broadcasted_iota(jnp.int32, scores.shape, 1) <= lax.rem(row, tokens)
    scores = jnp.where(allowed, scores, -1e30)
    peak = jnp.max(scores, axis=1, keepdims=True)
    weights = jnp.where(allowed, jnp.exp(scores - peak), 0.0)
    top[...] = peak
    norm[...] = jnp.sum(weights, axis=1, keepdims=True)
    acc[...] = mm_t(weights.astype(jnp.bfloat16), lat)

    second, third = 2, 4

    def block_of(s):
        share_keys(s, core, k2_s, k2_r, core).wait_recv()
        share_keys(s, diagonal, k4_s, k4_r, core).wait_recv()
        lat = keys[s, :, :lat_part, :].reshape(lat_width, tokens)
        return lat, keys[s, :, lat_part:, :].reshape(rope_width, tokens)

    def absorb(lat, rope):
        scores = scores_of(lat, rope)
        before = top[...]
        peak = jnp.maximum(before, jnp.max(scores, axis=1, keepdims=True))
        weights = jnp.exp(scores - peak)
        rescale = jnp.exp(before - peak)
        top[...] = peak
        norm[...] = norm[...] * rescale + jnp.sum(weights, axis=1, keepdims=True)
        acc[...] = acc[...] * rescale + mm_t(weights.astype(jnp.bfloat16), lat)

    def key_step(t, _):
        @pl.when(t <= c)
        def _():
            s, column = source_at(t)
            relay(s).wait_recv()

            @pl.when(column)
            def _():
                relay(s).start()
                relay_across(s).start()
                share_keys(s, h, k3_s, k3_r, across).start()

            share_keys(s, h, k2_s, k2_r, core).start()

        @pl.when((t > second) & (t <= c + second))
        def _():
            s, _ = source_at(t - second)
            share_keys(s, across, k3_s, k3_r, across).wait_recv()
            share_keys(s, across, k4_s, k4_r, core).start()

        w = t - third - y

        @pl.when((w == 0) & (y == 1))
        def _():
            absorb(*block_of(c - 1))

        @pl.when((w > 0) & (lax.rem(w, 2) == 0))
        def _():
            first, _ = source_at(t - third - 1)
            then, _ = source_at(t - third)
            blocks = zip(block_of(first), block_of(then))
            absorb(*[jnp.concatenate(pair, axis=1) for pair in blocks])

        return 0

    lax.fori_loop(1, c + 1 + third, key_step, 0)
    head_latent = (acc[...] / norm[...]).astype(jnp.bfloat16)
    loads[0].wait()
    loads[1].wait()
    head_value = jnp.concatenate(
        [
            mm(head_latent[a * tokens : (a + 1) * tokens, :], wv[a]).astype(jnp.bfloat16)
            for a in range(heads)
        ],
        axis=1,
    )

    def to_core(k):
        return remote(psend.at[k], ra.at[k], ra_s.at[k], ra_r.at[k], c, core)

    def to_across():
        return remote(rb_send, rb_recv, rb_s.at[0], rb_r.at[0], c, across)

    def dispatch(to):
        return remote(outgoing.at[to], arrived.at[h, c], d_s.at[to], d_r.at[c], to, h)

    def arrival(s):
        return remote(outgoing.at[s], arrived.at[h, s], d_s.at[s], d_r.at[s], s, h)

    def share_rows(j, g, send, recv, hd):
        part = arrived.at[g, pl.ds(j * per, per)]
        return remote(part, part, send.at[j], recv.at[j], c, hd)

    def take_chunk(j):
        def landed(k, _):
            i = j * per + k

            @pl.when(i != c)
            def _():
                arrival(i).wait_recv()

            return 0

        lax.fori_loop(0, per, landed, 0)
        share_rows(j, h, f2_s, f2_r, across).start()
        share_rows(j, h, f1_s, f1_r, core).start()

    def pass_chunk(j):
        share_rows(j, across, f2_s, f2_r, across).wait_recv()
        share_rows(j, across, f3_s, f3_r, core).start()

    mine = c // per
    mate = mine + 1 - 2 * lax.rem(mine, 2)

    def turn(p):
        if chunks < 8:
            return p
        third_pair = jnp.where(p == 2, mine, jnp.where(p == 3, mate, p - 2))
        last_pair = jnp.where(p == 3, mate, jnp.where(p == chunks - 1, mine, p - (p > 3).astype(jnp.int32)))
        third_pair = jnp.where(p >= 6, p - 4, jnp.where(p >= 4, p + 2, third_pair))
        third_pair = jnp.where(p < 2, p, third_pair)
        last_pair = jnp.where(p < 2, p, last_pair)
        order = jnp.where(mine >= 6, last_pair, third_pair)
        return jnp.where(mine >= 4, order, p)

    late = c // per >= chunks - 2
    lead = 2 * late.astype(jnp.int32)

    psend[1] = mm(head_value, wo[:, cols(diagonal)]).astype(jnp.bfloat16)
    to_core(1).start()
    across_part = mm(head_value, wo[:, cols(across)])
    to_core(1).wait_recv()
    rb_send[...] = (across_part + ra[1].astype(f32)).astype(jnp.bfloat16)
    to_across().start()
    psend[0] = mm(head_value, wo[:, cols(core)]).astype(jnp.bfloat16)
    to_core(0).start()
    own_part = mm(head_value, wo[:, cols(h)])
    width = (n + 127) // 128 * 128
    lane = lax.broadcasted_iota(jnp.int32, (tokens, width), 1)
    below = (
        lax.broadcasted_iota(jnp.int32, (tokens, tokens), 0)
        > lax.broadcasted_iota(jnp.int32, (tokens, tokens), 1)
    ).astype(f32).astype(jnp.bfloat16)
    earlier = lane.astype(f32) * cap
    places, place_rows, gates = [], [], []

    def column(ref, k):
        line = ref[k : k + 1, :].astype(f32)
        return jnp.transpose(jnp.broadcast_to(line, (128, tokens)))[:, :1]

    entries = lax.broadcasted_iota(jnp.int32, (tokens, table.shape[1]), 1)
    for k in range(ids.shape[0]):
        member = (column(ids, k) == lane.astype(f32)).astype(f32)
        rank = mm(below, member.astype(jnp.bfloat16)) + earlier
        place = jnp.sum(member * rank, axis=1, keepdims=True)
        earlier = earlier + jnp.sum(member, axis=0, keepdims=True)
        places.append(place)
        place_rows.append(jnp.transpose(jnp.broadcast_to(place, (tokens, 128)))[:1, :])
        chosen = column(gate_index, k) == entries.astype(f32)
        gates.append(jnp.sum(jnp.where(chosen, table[...], 0.0), axis=1, keepdims=True))

    def find_rows(e, _):
        slot = (lax.broadcasted_iota(jnp.int32, (cap, tokens), 0) + e * cap).astype(f32)
        hit = jnp.zeros((cap, tokens), f32)
        for row in place_rows:
            hit = hit + (slot == row).astype(f32)
        hits[pl.ds(pl.multiple_of(e * cap, cap), cap), :] = hit.astype(jnp.bfloat16)
        return 0

    lax.fori_loop(0, n, find_rows, 0)
    slot = lax.broadcasted_iota(jnp.int32, (tokens, n * cap), 1).astype(f32)
    for k, place in enumerate(places):
        picks[k] = (slot == place).astype(f32).astype(jnp.bfloat16)
        gate_of[k] = gates[k]
    loads[2].wait()
    to_core(0).wait_recv()
    base = hidden[:, cols(h)].astype(f32) + (own_part + ra[0].astype(f32))

    @pl.when(late)
    def _():
        take_chunk(0)
        take_chunk(1)

    to_across().wait_recv()
    attended = base + rb_recv[...].astype(f32)
    att[...] = attended
    scaled = (attended * gain[:, cols(h)]).astype(jnp.bfloat16)

    outgoing[...] = mm(hits[...], scaled).astype(jnp.bfloat16).reshape(n, cap, share)

    def send_rows(k, _):
        @pl.when(k != c)
        def _():
            dispatch(k).start()

        return 0

    held = c // per >= chunks - 2

    @pl.when(held)
    def _():
        lax.fori_loop(n // 2, n, send_rows, 0)

    upward = (c >= n // 4) & (c < n // 2)

    @pl.when(upward)
    def _():
        lax.fori_loop(0, n // 2, lambda k, _: send_rows(n // 2 + k, _), 0)

    lax.fori_loop(0, n // 2, send_rows, 0)

    @pl.when(jnp.logical_not(held | upward))
    def _():
        lax.fori_loop(n // 2, n, send_rows, 0)

    arrived[h, c] = outgoing[c]

    def y_core(j):
        return remote(ysend.at[j, 0], yrecv.at[j, 0], y_s.at[j], y_r.at[j], c, core)

    def y_diagonal(j):
        return remote(ysend.at[j, 1], yrecv.at[j, 1], yd_s.at[j], yd_r.at[j], c, core)

    def y_across(j):
        return remote(xsend.at[j], xrecv.at[j], x_s.at[j], x_r.at[j], c, across)

    def give_back(s):
        return remote(back.at[s], returned.at[c], b_s.at[s], b_r.at[c], s, h)

    def come_home(e):
        return remote(back.at[e], returned.at[e], b_s.at[e], b_r.at[e], e, h)

    inverse_gain = 1.0 / gain[...]
    inverse_gain = inverse_gain * inverse_gain

    def step(t, _):
        @pl.when((t + 3 >= lead) & (t + 3 < chunks))
        def _():
            take_chunk(turn(t + 3))

        @pl.when((t + 1 >= 0) & (t + 1 < chunks))
        def _():
            pass_chunk(turn(t + 1))

        @pl.when((t >= 0) & (t < chunks))
        def _():
            j = turn(t)
            share_rows(j, core, f1_s, f1_r, core).wait_recv()
            share_rows(j, diagonal, f3_s, f3_r, core).wait_recv()
            shares = [
                arrived[g, pl.ds(j * per, per)].reshape(per * cap, share) for g in range(hd_count)
            ]
            squares = jnp.zeros((per * cap, share), f32)
            for g, rows in enumerate(shares):
                wide = rows.astype(f32)
                squares = squares + wide * wide * inverse_gain[:, g * share : (g + 1) * share]
            rows = jnp.concatenate(shares, axis=1)
            gate_part = mm_t(rows, wg[...])
            up_part = mm_t(rows, wu[...])
            mean = jnp.sum(squares, axis=1, keepdims=True) / model_width
            inverse = lax.rsqrt(mean + 1e-06)
            gate_part = gate_part * inverse
            up_part = up_part * inverse
            units = (gate_part / (1.0 + jnp.exp(-gate_part)) * up_part).astype(jnp.bfloat16)
            ysend[j, 1] = mm(units, wd[:, cols(diagonal)]).astype(jnp.bfloat16)
            y_diagonal(j).start()
            yown[j, 1] = mm(units, wd[:, cols(across)])
            ysend[j, 0] = mm(units, wd[:, cols(core)]).astype(jnp.bfloat16)
            y_core(j).start()
            y_diagonal(j).wait_recv()
            xsend[j] = (yown[j, 1] + yrecv[j, 1].astype(f32)).astype(jnp.bfloat16)
            y_across(j).start()
            yown[j, 0] = mm(units, wd[:, cols(h)])

        @pl.when(t >= 1)
        def _():
            j = turn(t - 1)
            y_core(j).wait_recv()
            y_across(j).wait_recv()
            whole = yown[j, 0] + yrecv[j, 0].astype(f32) + xrecv[j].astype(f32)
            back[pl.ds(j * per, per)] = whole.astype(jnp.bfloat16).reshape(per, cap, share)

            def go(k, _):
                i = j * per + k

                @pl.when(i != c)
                def _():
                    give_back(i).start()

                return 0

            lax.fori_loop(0, per, go, 0)

        return 0

    for load in loads[3:]:
        load.wait()
    lax.fori_loop(-3, chunks + 1, step, 0)
    returned[c] = back[c]

    def home(i, _):
        come_home(lax.rem(c + i, n)).wait_recv()
        return 0

    lax.fori_loop(1, n, home, 0)
    rows = returned[...].reshape(n * cap, share)
    mixed = att[...]
    for k in range(len(places)):
        mixed = mixed + gate_of[k] * mm(picks[k], rows)
    out[...] = mixed.astype(out.dtype)

    def sent_keys(k, _):
        to_column(k).wait_send()
        return 0

    def sent_relays(k, _):
        s = 2 * k + y
        relay(s).wait_send()
        relay_across(s).wait_send()
        share_keys(s, h, k3_s, k3_r, across).wait_send()
        return 0

    def sent_shares(i, _):
        share_keys(i, h, k2_s, k2_r, core).wait_send()
        share_keys(i, across, k4_s, k4_r, core).wait_send()
        return 0

    @pl.when(y == 0)
    def _():
        to_partner().wait_send()
        second_to_partner().wait_send()

    lax.fori_loop(z + 1, n // 2, sent_keys, 0)
    lax.fori_loop(0, z, sent_relays, 0)
    lax.fori_loop(0, c, sent_shares, 0)
    to_core(0).wait_send()
    to_core(1).wait_send()
    to_across().wait_send()

    def sent(i, _):
        to = lax.rem(c + i, n)
        give_back(to).wait_send()
        dispatch(to).wait_send()
        return 0

    lax.fori_loop(1, n, sent, 0)

    def sent_chunk(j, _):
        share_rows(j, h, f1_s, f1_r, core).wait_send()
        share_rows(j, h, f2_s, f2_r, across).wait_send()
        share_rows(j, across, f3_s, f3_r, core).wait_send()
        y_core(j).wait_send()
        y_diagonal(j).wait_send()
        y_across(j).wait_send()
        return 0

    lax.fori_loop(0, chunks, sent_chunk, 0)


def on_device(
    hidden_in,
    q_latent,
    q_rotary,
    latent,
    k_rotary,
    w_value,
    w_output,
    ffn_gain,
    w_gate,
    w_up,
    w_down,
    expert_ids,
    gate_index,
    gate_table,
):
    n, hd_count = lax.axis_size("ctx"), lax.axis_size("hd")
    tokens, width = hidden_in.shape
    share = width // hd_count
    needed = 3 * tokens * expert_ids.shape[1] // (2 * n * w_gate.shape[0])
    cap = (needed + 15) // 16 * 16
    chunks = math.gcd(n, 8)
    rows = n // chunks * cap
    bf = jnp.bfloat16
    f32 = jnp.float32
    vm = pltpu.VMEM
    lat_width, rope_width = latent.shape[0], k_rotary.shape[0]
    stacked = w_value.shape[0] * tokens
    quarter = (lat_width + rope_width) // hd_count
    return pl.pallas_call(
        functools.partial(layer_kernel, n, chunks, width),
        out_shape=jax.ShapeDtypeStruct((tokens, share), bf),
        in_specs=[pl.BlockSpec(memory_space=pltpu.VMEM)] * 5
        + [pl.BlockSpec(memory_space=pl.ANY)] * 9,
        out_specs=pl.BlockSpec(memory_space=pltpu.VMEM),
        scratch_shapes=[
            vm(hidden_in.shape, bf),
            vm(w_value.shape, bf),
            vm(w_output.shape, bf),
            vm(w_gate.shape[:0:-1], bf),
            vm(w_up.shape[:0:-1], bf),
            vm(w_down.shape[1:], bf),
            vm((hd_count, quarter, tokens), bf),
            vm((n, hd_count, quarter, tokens), bf),
            vm((stacked, lat_width), bf),
            vm((stacked, rope_width), bf),
            vm((stacked, 1), f32),
            vm((stacked, 1), f32),
            vm((stacked, lat_width), f32),
            vm((n * cap, tokens), bf),
            vm((expert_ids.shape[1], tokens, n * cap), bf),
            vm((expert_ids.shape[1], tokens, 1), f32),
            vm((2, tokens, share), bf),
            vm((2, tokens, share), bf),
            vm((tokens, share), bf),
            vm((tokens, share), bf),
            vm((tokens, share), f32),
            vm((n, cap, share), bf),
            vm((hd_count, n, cap, share), bf),
            vm((chunks, 2, rows, share), f32),
            vm((chunks, 2, rows, share), bf),
            vm((chunks, 2, rows, share), bf),
            vm((chunks, rows, share), bf),
            vm((chunks, rows, share), bf),
            vm((n, cap, share), bf),
            vm((n, cap, share), bf),
        ]
        + [DMA((2 * hd_count + w_value.shape[0],)), DMA((6,)), DMA((1,))]
        + [DMA((n,))] * 10
        + [DMA((2,))] * 2
        + [DMA((1,))] * 2
        + [DMA((n,))] * 2
        + [DMA((chunks,))] * 12
        + [DMA((n,))] * 2,
        compiler_params=pltpu.CompilerParams(
            collective_id=0, has_side_effects=True, vmem_limit_bytes=60 * 1024 * 1024
        ),
    )(
        q_rotary,
        ffn_gain[None, :],
        expert_ids.T,
        gate_index.T,
        gate_table[None, :],
        q_latent,
        latent,
        k_rotary,
        hidden_in,
        w_value,
        w_output,
        jnp.swapaxes(w_gate, 1, 2),
        jnp.swapaxes(w_up, 1, 2),
        w_down,
    )


def solution(mesh):
    in_specs = (
        P("ctx", None),
        P("ctx", "hd"),
        P("ctx", "hd"),
        P(None, "ctx"),
        P(None, "ctx"),
        P("hd", None, None),
        P("hd", None),
        P(),
        P("ctx", None, "hd"),
        P("ctx", None, "hd"),
        P("ctx", "hd", None),
        P("ctx", None),
        P("ctx", None),
        P(),
    )
    out_specs = P("ctx", "hd")
    return jax.shard_map(
        on_device, mesh=mesh, in_specs=in_specs, out_specs=out_specs, check_vma=False
    )
```
